32 devices in a mesh: groups: 2 (over y), seq: 4 (over z), rep: 4 (over x, core).
Axes of the slice: x: 2, y: 2, z: 4, core: 2. Of those that a mesh axis runs over, the one named last changes fastest.
Arguments:
- points: bfloat16 [65536, 256], P(('groups', 'seq', 'rep')), parts along dimension 0, may hold values from -8 to 8
- ball_order: int32 [32, 2048], P(('groups', 'seq', 'rep')), parts along dimension 0, may hold values from 0 to 2047, as said below
- ball_counts: int32 [512], P(('groups', 'seq', 'rep')), parts along dimension 0, may hold values from 1 to 128
- gain_attn: float32 [256], replicated, may hold values from 0.25 to 1.75
- gain_mlp: float32 [256], replicated, may hold values from 0.25 to 1.75
- head_temps: float32 [2, 8], replicated, may hold values from 2 to 6
- w_qkv: bfloat16 [256, 768], replicated, may hold values from -0.375 to 0.375
- w_out: bfloat16 [256, 256], replicated, may hold values from -0.375 to 0.375
- c_qkv: bfloat16 [256, 768], replicated, may hold values from -0.375 to 0.375
- c_out: bfloat16 [256, 256], replicated, may hold values from -0.375 to 0.375
- w_up: bfloat16 [256, 1024], replicated, may hold values from -0.375 to 0.375
- w_down: bfloat16 [1024, 256], replicated, may hold values from -0.1875 to 0.1875
Outputs:
- layer_out: bfloat16 [65536, 256], P(('groups', 'seq', 'rep')), parts along dimension 0
The draws below stay inside these ranges and needn't reach their ends.
There are 2 independent parts, one for each index of `groups`. The reference program is written for one: setup_inputs(seed, part) draws one part's arguments, and reference() takes and returns one part's arrays. A program takes and returns all parts, laid end to end along the dimension named above; an argument that names none is the same for every part. Nothing has to cross between parts.
Inputs may be any that keep to these rules, and one draw needn't show every extreme that they name: `ball_order`: each row is a permutation of 0 to 2047: for every ball-ordered position of a device's block, the row of that block in stored order. `ball_counts`: valid points of each ball of 128 consecutive ball-ordered rows; the valid ones come first.
All inputs are finite; a program needn't handle non-finite values.
Results may differ from the reference program's by a relative error of at most 0.009.
Values may be sent and summed in bfloat16 or wider, within the bound.
A program may use at most 128 MiB of HBM per device.

```python
import math
import jax
import jax.numpy as jnp
from jax import lax

D = 256
HEADS = 8
FFN = 1024
BALL = 128
POOL = 64
TOK_DEV = 2048
BLOCKS = 16
POINTS = 32768
BALLS = 256
COARSE = 512


def shuffle_block(block_key):
    return jax.random.permutation(block_key, TOK_DEV)


def ball_permutations(key):
    block_keys = jax.random.split(jax.random.fold_in(key, 11), BLOCKS)
    return jax.vmap(shuffle_block)(block_keys).astype(jnp.int32)


def draw_ball_order(key, part):
    return ball_permutations(key)


def draw_points(key, part):
    order = ball_permutations(key)
    offset_key = jax.random.fold_in(key, 23)
    noise_key = jax.random.fold_in(key, 29)
    offsets = 1.5 * jax.random.normal(offset_key, (COARSE, D), jnp.float32)
    noise = jax.random.normal(noise_key, (POINTS, D), jnp.float32)
    ordered = (jnp.repeat(offsets, POOL, axis=0) + noise).reshape(BLOCKS, TOK_DEV, D)
    block_index = jnp.arange(BLOCKS, dtype=jnp.int32)[:, None]
    stored = jnp.zeros((BLOCKS, TOK_DEV, D), jnp.float32).at[block_index, order].set(ordered)
    return jnp.clip(stored.reshape(POINTS, D), -8.0, 8.0).astype(jnp.bfloat16)


def set_ends(array, stream_key, low, high):
    extent = array.shape
    place = [jax.random.randint(jax.random.fold_in(stream_key, axis), (), 0, extent[axis]) for axis in range(len(extent))]
    array = array.at[tuple(place)].set(low)
    longest = extent.index(max(extent))
    place[longest] = (place[longest] + 1) % extent[longest]
    return array.at[tuple(place)].set(high)


def normal_values(rng, extent, deviation, bound, held_as=jnp.bfloat16):
    return jnp.clip(deviation * jax.random.normal(rng, extent, jnp.float32), -bound, bound).astype(held_as)


def setup_inputs(seed: int = 0, part: int = 0) -> dict:
    key_of = jax.random.split(jax.random.key(seed), 13)
    part_splits = jax.random.split(jax.random.fold_in(key_of[12], part), 13)
    points = draw_points(jax.random.fold_in(jax.random.fold_in(key_of[12], part), 71), part)
    ball_order = draw_ball_order(jax.random.fold_in(jax.random.fold_in(key_of[12], part), 71), part)
    ball_counts = set_ends(jax.random.randint(part_splits[2], (BALLS,), 1, BALL + 1), jax.random.fold_in(part_splits[2], 1), 1, BALL).astype(jnp.int32)
    gain_attn = jnp.clip(1.0 + 0.15 * jax.random.normal(key_of[3], (D,), jnp.float32), 0.25, 1.75)
    gain_mlp = jnp.clip(1.0 + 0.15 * jax.random.normal(key_of[4], (D,), jnp.float32), 0.25, 1.75)
    head_temps = jnp.clip(jnp.exp(jax.random.uniform(key_of[5], (2, HEADS), jnp.float32, math.log(2.0), math.log(6.0))), 2.0, 6.0)
    w_qkv = normal_values(key_of[6], (D, 3 * D), D ** -0.5, 0.375)
    w_out = normal_values(key_of[7], (D, D), D ** -0.5, 0.375)
    c_qkv = normal_values(key_of[8], (D, 3 * D), D ** -0.5, 0.375)
    c_out = normal_values(key_of[9], (D, D), D ** -0.5, 0.375)
    w_up = normal_values(key_of[10], (D, FFN), D ** -0.5, 0.375)
    w_down = normal_values(key_of[11], (FFN, D), FFN ** -0.5, 0.1875)
    return dict(points=points, ball_order=ball_order, ball_counts=ball_counts, gain_attn=gain_attn, gain_mlp=gain_mlp, head_temps=head_temps, w_qkv=w_qkv, w_out=w_out, c_qkv=c_qkv, c_out=c_out, w_up=w_up, w_down=w_down)


def rms_norm(source, gain):
    values = source.astype(jnp.float32)
    scaled = values * lax.rsqrt(lax.optimization_barrier(jnp.mean(values * values, axis=-1, keepdims=True)) + 1e-06)
    return (scaled * gain).astype(jnp.bfloat16)

def head_norm(source):
    values = source.astype(jnp.float32)
    return (values * lax.rsqrt(lax.optimization_barrier(jnp.mean(values * values, axis=-1, keepdims=True)) + 1e-06)).astype(jnp.bfloat16)

def to_wide(source):
    return lax.optimization_barrier(source).astype(jnp.float32)

def split_heads(joined, heads):
    shaped = joined.reshape(joined.shape[0], 3, heads, -1)
    return (shaped[:, 0], shaped[:, 1], shaped[:, 2])

def ball_attend(q_norm, k_norm, values, counts, temps):
    rows, heads, head_dim = q_norm.shape
    ball_total = rows // BALL
    per_group = math.gcd(ball_total, max(1, 512 // BALL))
    group_total = ball_total // per_group
    shape = (group_total, per_group, BALL, heads, head_dim)
    scale = temps / math.sqrt(head_dim)

    def one_group(block):
        query_blk, key_blk, value_blk, count_blk = block
        scores = jnp.einsum('bqhd,bkhd->bhqk', to_wide(query_blk), to_wide(key_blk)) * scale[None, :, None, None]
        valid = (jnp.arange(BALL)[None, :] < count_blk[:, None]).astype(jnp.float32)
        weights = jnp.exp(scores) * valid[:, None, None, :]
        probs_half = (weights / lax.optimization_barrier(jnp.sum(weights, axis=-1, keepdims=True))).astype(jnp.bfloat16)
        mixed = jnp.einsum('bhqk,bkhd->bqhd', to_wide(probs_half), to_wide(value_blk))
        return mixed.astype(jnp.bfloat16)
    result = lax.map(one_group, (q_norm.reshape(shape), k_norm.reshape(shape), values.reshape(shape), counts.reshape(group_total, per_group)))
    return result.reshape(rows, heads * head_dim)

def reference(points, ball_order, ball_counts, gain_attn, gain_mlp, head_temps, w_qkv, w_out, c_qkv, c_out, w_up, w_down):
    heads = head_temps.shape[1]
    width = points.shape[1]
    head_dim = width // heads
    blocked = points.reshape(BLOCKS, TOK_DEV, width)
    sorted_rows = jnp.take_along_axis(blocked, ball_order[:, :, None].astype(jnp.int32), axis=1).reshape(POINTS, width)
    normed = rms_norm(sorted_rows, gain_attn)
    joined = jnp.dot(normed, w_qkv, preferred_element_type=jnp.float32).astype(jnp.bfloat16)
    queries, key_rows, values = split_heads(joined, heads)
    fine_mix = ball_attend(head_norm(queries), head_norm(key_rows), values, ball_counts, head_temps[0])
    fine_term = jnp.dot(fine_mix, w_out, preferred_element_type=jnp.float32)
    halves = BALL // POOL
    half_count = jnp.clip(ball_counts[:, None] - POOL * jnp.arange(halves, dtype=jnp.int32)[None, :], 0, POOL).reshape(COARSE)
    row_mask = (jnp.arange(POOL)[None, :] < half_count[:, None]).astype(jnp.float32)
    summed = lax.optimization_barrier(jnp.sum(normed.astype(jnp.float32).reshape(COARSE, POOL, width) * row_mask[:, :, None], axis=1))
    pooled = (summed / jnp.maximum(half_count, 1).astype(jnp.float32)[:, None]).astype(jnp.bfloat16)
    coarse_joined = jnp.dot(pooled, c_qkv, preferred_element_type=jnp.float32).astype(jnp.bfloat16)
    c_queries, c_keys, c_values = split_heads(coarse_joined, heads)
    cq_norm = head_norm(c_queries)
    ck_norm = to_wide(head_norm(c_keys))
    cv_wide = c_values.astype(jnp.float32)
    key_mask = (half_count > 0).astype(jnp.float32)
    scale = head_temps[1] / math.sqrt(head_dim)
    per_block = math.gcd(COARSE, 512)

    def query_block(block):
        scores = jnp.einsum('qhd,khd->hqk', to_wide(block), ck_norm) * scale[:, None, None]
        weights = jnp.exp(scores) * key_mask[None, None, :]
        numer = jnp.einsum('hqk,khd->qhd', to_wide(weights.astype(jnp.bfloat16)), cv_wide)
        denom = lax.optimization_barrier(jnp.sum(weights, axis=-1)).T
        return (numer / denom[:, :, None]).reshape(block.shape[0], width).astype(jnp.bfloat16)
    coarse_mix = lax.map(query_block, cq_norm.reshape(COARSE // per_block, per_block, heads, head_dim)).reshape(COARSE, width)
    coarse_term = jnp.dot(coarse_mix, c_out, preferred_element_type=jnp.float32)
    unpooled = jnp.repeat(coarse_term, POOL, axis=0)
    middle = (sorted_rows.astype(jnp.float32) + fine_term + unpooled).astype(jnp.bfloat16)
    mlp_in = rms_norm(middle, gain_mlp)
    upward = jnp.dot(mlp_in, w_up, preferred_element_type=jnp.float32)
    activated = jax.nn.gelu(upward, approximate=True).astype(jnp.bfloat16)
    downward = jnp.dot(activated, w_down, preferred_element_type=jnp.float32)
    result_rows = (middle.astype(jnp.float32) + downward).astype(jnp.bfloat16)
    block_index = jnp.arange(BLOCKS, dtype=jnp.int32)[:, None]
    placed = jnp.zeros((BLOCKS, TOK_DEV, width), jnp.bfloat16).at[block_index, ball_order.astype(jnp.int32)].set(result_rows.reshape(BLOCKS, TOK_DEV, width))
    return placed.reshape(POINTS, width)
```

```python
import functools
import math

import jax
import jax.numpy as jnp
from jax import lax
from jax.experimental import pallas as pl
from jax.experimental.pallas import tpu as pltpu
from jax.sharding import PartitionSpec as P

BALL = 128
POOL = 64
EPS = 1e-06
VMEM_ATTEND = 61 << 20
VMEM_MLP = 61 << 20
LANES = 128
GELU_A = math.sqrt(2.0 / math.pi)
GELU_B = 0.044715 * math.sqrt(2.0 / math.pi)
LOG2E = 1.4426950408889634
MESH = pl.DeviceIdType.MESH
BF = jnp.bfloat16
F32 = jnp.float32


def dot(a, b):
    return jnp.dot(a, b, preferred_element_type=F32)


def dot_t(a, b):
    return lax.dot_general(a, b, (((1,), (1,)), ((), ())), preferred_element_type=F32)


def gelu_of_half(half):
    inner = half * (2.0 * GELU_A + 8.0 * GELU_B * (half * half))
    return half + half * jnp.tanh(inner)


def rms(values, gain):
    return values * lax.rsqrt(jnp.mean(values * values, axis=-1, keepdims=True) + EPS) * gain


def attend_kernel(
    sizes,
    points,
    order,
    counts,
    gain_attn,
    temps,
    w_qkv_hbm,
    w_out_hbm,
    c_qkv_hbm,
    c_out_hbm,
    mid_out,
    coarse,
    srt,
    nrm,
    mid,
    stage,
    tokens_all,
    w_qkv,
    w_out,
    c_qkv,
    c_out,
    load_sem,
    out_sem,
    local_sem,
    seq_send,
    rep_send,
    recv_sem,
):
    seq_n, rep_n, heads = sizes
    peers = seq_n * rep_n
    rows, width = points.shape
    head_dim = width // heads
    chunk = 4 * BALL
    chunks = rows // chunk
    tokens = chunk // POOL
    coarse_rows = rows // POOL
    my_seq = lax.axis_index("seq")
    my_rep = lax.axis_index("rep")
    me = my_seq * rep_n + my_rep

    loads = [
        pltpu.make_async_copy(source, target, load_sem.at[n])
        for n, (source, target) in enumerate(
            [(w_qkv_hbm, w_qkv), (w_out_hbm, w_out), (c_qkv_hbm, c_qkv), (c_out_hbm, c_out)]
        )
    ]
    for load in loads:
        load.start()

    barrier = pltpu.get_barrier_semaphore()

    def greet_seq(step, carry):
        place = {"seq": lax.rem(my_seq + step, seq_n), "rep": my_rep}
        pl.semaphore_signal(barrier, inc=1, device_id=place, device_id_type=MESH)
        return carry

    def greet_rep(step, carry):
        place = {"seq": my_seq, "rep": lax.rem(my_rep + step, rep_n)}
        pl.semaphore_signal(barrier, inc=1, device_id=place, device_id_type=MESH)
        return carry

    lax.fori_loop(1, seq_n, greet_seq, 0)
    lax.fori_loop(1, rep_n, greet_rep, 0)

    lane_head = lax.broadcasted_iota(jnp.int32, (1, width), 1) // head_dim
    near_heads = LANES // head_dim
    slabs = [slice(g * LANES, (g + 1) * LANES) for g in range(width // LANES)]
    near = lax.broadcasted_iota(jnp.int32, (1, LANES), 1) // head_dim
    head_lanes = [(near == h).astype(F32).astype(BF) for h in range(near_heads)]

    def by_head(block):
        return jnp.concatenate([block * lanes for lanes in head_lanes], axis=0)

    block_mean = jnp.where(
        lax.broadcasted_iota(jnp.int32, (width, width), 0) // head_dim
        == lax.broadcasted_iota(jnp.int32, (width, width), 1) // head_dim,
        1.0 / head_dim,
        0.0,
    ).astype(BF)

    def lane_scale(row):
        scale = jnp.zeros((1, width), F32)
        for h in range(heads):
            scale = jnp.where(lane_head == h, temps[row, h], scale)
        return scale * (LOG2E / math.sqrt(head_dim))

    def head_rms(values):
        return values * lax.rsqrt(dot((values * values).astype(BF), block_mean) + EPS)

    gain_a = gain_attn[...]

    def gather_chunk(i, carry):
        base = pl.multiple_of(i * chunk, chunk)
        picks = []
        lane = lax.broadcasted_iota(jnp.int32, (BALL, BALL), 1).astype(F32)
        for b in range(4):
            row = order[:, pl.ds(base + b * BALL, BALL)].astype(F32)
            column = jnp.transpose(jnp.broadcast_to(row, (BALL, BALL)))
            picks.append(
                jnp.concatenate(
                    [
                        jnp.where(column == lane + float(j * BALL), 1.0, 0.0).astype(BF)
                        for j in range(rows // BALL)
                    ],
                    axis=1,
                )
            )
        sorted_rows = dot(jnp.concatenate(picks, axis=0), points[...])
        srt[pl.ds(base, chunk), :] = sorted_rows.astype(BF)
        normed = rms(sorted_rows, gain_a).astype(BF)
        nrm[pl.ds(base, chunk), :] = normed
        shape = (2 * tokens, chunk)
        token = lax.broadcasted_iota(jnp.int32, shape, 0)
        place = lax.broadcasted_iota(jnp.int32, shape, 1)
        half = jnp.zeros(shape, jnp.int32)
        for b in range(4):
            half = jnp.where(token // 2 == b, counts[i * 4 + b], half)
        half = jnp.clip(half - POOL * (token % 2), 0, POOL)
        offset = place - token * POOL
        take = jnp.where((offset >= 0) & (offset < half), 1.0, 0.0).astype(BF)
        total = dot(take, normed)[:tokens]
        half_f = half[:tokens, :width].astype(F32)
        spot = pl.ds(pl.multiple_of(i * tokens, tokens), tokens)
        stage[spot, :width] = total / jnp.maximum(half_f, 1.0)
        stage[spot, width:] = jnp.where(half_f[:, :128] > 0.0, 1.0, 0.0)
        return carry

    lax.fori_loop(0, chunks, gather_chunk, 0)

    own_block = stage[...].astype(BF)
    tokens_all[me] = own_block

    pl.semaphore_wait(barrier, seq_n + rep_n - 2)

    def seq_copy(step):
        return pltpu.make_async_remote_copy(
            src_ref=tokens_all.at[me],
            dst_ref=tokens_all.at[me],
            send_sem=seq_send.at[step],
            recv_sem=recv_sem.at[me],
            device_id={"seq": lax.rem(my_seq + step, seq_n), "rep": my_rep},
            device_id_type=MESH,
        )

    def rep_copy(away, step):
        block = lax.rem(my_seq + away, seq_n) * rep_n + my_rep
        return pltpu.make_async_remote_copy(
            src_ref=tokens_all.at[block],
            dst_ref=tokens_all.at[block],
            send_sem=rep_send.at[away, step],
            recv_sem=recv_sem.at[block],
            device_id={"seq": my_seq, "rep": lax.rem(my_rep + step, rep_n)},
            device_id_type=MESH,
        )

    def arrival(block):
        return pltpu.make_async_remote_copy(
            src_ref=tokens_all.at[block],
            dst_ref=tokens_all.at[block],
            send_sem=seq_send.at[0],
            recv_sem=recv_sem.at[block],
            device_id={"seq": lax.rem(my_seq + 1, seq_n), "rep": my_rep},
            device_id_type=MESH,
        )

    def each(count, first, act):
        def body(step, carry):
            act(step)
            return carry

        lax.fori_loop(first, count, body, 0)

    each(seq_n, 1, lambda step: seq_copy(step).start())
    each(rep_n, 1, lambda step: rep_copy(0, step).start())

    def relay(away):
        arrival(lax.rem(my_seq + away, seq_n) * rep_n + my_rep).wait_recv()
        each(rep_n, 1, lambda step: rep_copy(away, step).start())

    for load in loads:
        load.wait()

    q_scale = lane_scale(0)

    def ball_chunk(i, carry):
        base = pl.multiple_of(i * chunk, chunk)
        spot = pl.ds(base, chunk)
        joined = dot(nrm[spot, :], w_qkv[...])
        q = (head_rms(joined[:, :width]) * q_scale).astype(BF)
        k = head_rms(joined[:, width : 2 * width]).astype(BF)
        v = joined[:, 2 * width :]
        mixes = []
        for b in range(4):
            part = slice(b * BALL, (b + 1) * BALL)
            live = lax.broadcasted_iota(jnp.int32, (BALL, width), 0) < counts[i * 4 + b]
            vb = jnp.where(live, v[part], 0.0).astype(BF)
            ones = by_head(jnp.where(live[:, :LANES], 1.0, 0.0).astype(BF))
            slab_mixes = []
            for slab in slabs:
                weights = jnp.exp2(dot_t(q[part, slab], by_head(k[part, slab]))).astype(BF)
                mixed = dot(weights, jnp.concatenate([by_head(vb[:, slab]), ones], axis=1))
                slab_mixes.append((mixed[:, :LANES] / mixed[:, LANES:]).astype(BF))
            mixes.append(jnp.concatenate(slab_mixes, axis=1))
        fine = dot(jnp.concatenate(mixes, axis=0), w_out[...])
        mid[spot, :] = (srt[spot, :].astype(F32) + fine).astype(BF)
        return carry

    def leave(i):
        spot = pl.ds(pl.multiple_of(i * chunk, chunk), chunk)
        return pltpu.make_async_copy(mid.at[spot, :], mid_out.at[spot, :], out_sem.at[i])

    def ball_step(i, carry):
        ball_chunk(i, carry)
        leave(i).start()
        return carry

    early = chunks // 2
    lax.fori_loop(0, early, ball_step, 0)
    each(seq_n, 1, relay)
    lax.fori_loop(early, chunks, ball_step, 0)

    q_c = dot(own_block[:, :width], c_qkv[:, :width])
    q_c = (head_rms(q_c) * lane_scale(1)).astype(BF)
    queries = [by_head(q_c[:, slab]) for slab in slabs]

    def gathered(step):
        def one(away):
            rep = lax.rem(my_rep + step, rep_n)
            arrival(lax.rem(my_seq + away, seq_n) * rep_n + rep).wait_recv()

        each(seq_n, 0, one)

    each(rep_n, 1, gathered)

    group = math.gcd(peers, 16)

    def coarse_keys(g):
        block = tokens_all[pl.ds(g * group, group)].reshape(group * coarse_rows, width + 128)
        joined = dot(block[:, :width], c_qkv[:, width:])
        keys = head_rms(joined[:, :width]).astype(BF)
        values = joined[:, width:].astype(BF)
        sums = []
        for query, slab in zip(queries, slabs):
            weights = jnp.exp2(dot_t(query, keys[:, slab])).astype(BF)
            sums.append(dot(weights, jnp.concatenate([values[:, slab], block[:, width:]], axis=1)))
        return sums

    if peers == group:
        sums = coarse_keys(0)
    else:
        sums = lax.fori_loop(
            0,
            peers // group,
            lambda g, total: [a + b for a, b in zip(total, coarse_keys(g))],
            [jnp.zeros((near_heads * coarse_rows, 2 * LANES), F32) for _ in slabs],
        )
    slab_mixes = []
    for total in sums:
        ratio = total[:, :LANES] / total[:, LANES:]
        mix = jnp.zeros((coarse_rows, LANES), F32)
        for h in range(near_heads):
            mix = jnp.where(near == h, ratio[h * coarse_rows : (h + 1) * coarse_rows], mix)
        slab_mixes.append(mix)
    mix = jnp.concatenate(slab_mixes, axis=1)
    coarse[...] = dot(mix.astype(BF), c_out[...])

    each(seq_n, 1, lambda step: seq_copy(step).wait_send())
    each(seq_n, 0, lambda away: each(rep_n, 1, lambda step: rep_copy(away, step).wait_send()))
    each(chunks, 0, lambda i: leave(i).wait())


def mlp_kernel(
    mid_hbm,
    coarse,
    order,
    gain_mlp,
    w_up_hbm,
    w_down_hbm,
    out,
    mid,
    w_up,
    w_down,
    res,
    ready,
    packed,
    order_twice,
    spots,
    mid_sem,
    load_sem,
    out_sem,
):
    rows, width = mid.shape
    chunk = 4 * BALL
    chunks = rows // chunk
    tokens = chunk // POOL
    gain_half = gain_mlp[...] * 0.5

    def enter(i):
        spot = pl.ds(i * chunk, chunk)
        return pltpu.make_async_copy(mid_hbm.at[spot, :], mid.at[spot, :], mid_sem.at[i])

    order_twice[...] = order[...] * 2
    load_up = pltpu.make_async_copy(w_up_hbm, w_up, load_sem.at[0])
    load_down = pltpu.make_async_copy(w_down_hbm, w_down, load_sem.at[1])
    load_spots = pltpu.make_async_copy(order_twice, spots, load_sem.at[2])
    enter(0).start()
    load_up.start()
    load_down.start()
    for i in range(1, chunks):
        enter(i).start()
    load_spots.start()
    load_up.wait()
    load_down.wait()

    def mlp_chunk(i):
        enter(i).wait()
        terms = coarse[pl.ds(i * tokens, tokens), :]
        spread = jnp.concatenate(
            [jnp.broadcast_to(terms[t : t + 1], (POOL, width)) for t in range(tokens)], axis=0
        )
        middle = mid[pl.ds(i * chunk, chunk), :].astype(F32) + spread
        mlp_in = rms(middle, gain_half).astype(BF)
        activated = gelu_of_half(dot(mlp_in, w_up[...]).astype(BF))
        result = middle + dot(activated, w_down[...])
        for n in range(width // LANES):
            res[pl.ds(2 * i * chunk + n, chunk, stride=2), :] = result[:, n * LANES : (n + 1) * LANES]

    def scatter_chunk(i):
        for r in range(i * chunk, (i + 1) * chunk):
            ready[pl.ds(spots[0, r], 2), :] = res[pl.ds(2 * r, 2), :]

    mlp_chunk(0)
    load_spots.wait()
    for i in range(1, chunks):
        scatter_chunk(i - 1)
        mlp_chunk(i)
    scatter_chunk(chunks - 1)

    def leave(i):
        spot = pl.ds(i * chunk, chunk)
        return pltpu.make_async_copy(packed.at[spot, :], out.at[spot, :], out_sem.at[i])

    for i in range(chunks):
        packed[pl.ds(i * chunk, chunk), :] = jnp.concatenate(
            [ready[pl.ds(2 * i * chunk + n, chunk, stride=2), :] for n in range(width // LANES)], axis=1
        ).astype(BF)
        leave(i).start()
    for i in range(chunks):
        leave(i).wait()


def on_device(
    sizes,
    points,
    ball_order,
    ball_counts,
    gain_attn,
    gain_mlp,
    head_temps,
    w_qkv,
    w_out,
    c_qkv,
    c_out,
    w_up,
    w_down,
):
    rows, width = points.shape
    heads = head_temps.shape[1]
    seq_n, rep_n = sizes
    peers = seq_n * rep_n
    coarse_rows = rows // POOL
    chunks = rows // (4 * BALL)
    vmem = pl.BlockSpec(memory_space=pltpu.VMEM)
    smem = pl.BlockSpec(memory_space=pltpu.SMEM)
    far = pl.BlockSpec(memory_space=pl.ANY)
    dma = pltpu.SemaphoreType.DMA
    mid, coarse = pl.pallas_call(
        functools.partial(attend_kernel, (*sizes, heads)),
        out_shape=(
            jax.ShapeDtypeStruct((rows, width), BF),
            jax.ShapeDtypeStruct((coarse_rows, width), F32),
        ),
        in_specs=[vmem, vmem, smem, vmem, smem] + [far] * 4,
        out_specs=(far, vmem),
        scratch_shapes=[
            pltpu.VMEM((rows, width), BF),
            pltpu.VMEM((rows, width), BF),
            pltpu.VMEM((rows, width), BF),
            pltpu.VMEM((coarse_rows, width + 128), F32),
            pltpu.VMEM((peers, coarse_rows, width + 128), BF),
            pltpu.VMEM(w_qkv.shape, BF),
            pltpu.VMEM(w_out.shape, BF),
            pltpu.VMEM(c_qkv.shape, BF),
            pltpu.VMEM(c_out.shape, BF),
            dma((4,)),
            dma((chunks,)),
            dma,
            dma((seq_n,)),
            dma((seq_n, rep_n)),
            dma((peers,)),
        ],
        compiler_params=pltpu.CompilerParams(
            collective_id=0, has_side_effects=True, vmem_limit_bytes=VMEM_ATTEND
        ),
        name="attend",
    )(
        points,
        ball_order,
        ball_counts,
        gain_attn.reshape(1, width),
        head_temps,
        w_qkv,
        w_out,
        c_qkv,
        c_out,
    )
    return pl.pallas_call(
        mlp_kernel,
        out_shape=jax.ShapeDtypeStruct(points.shape, points.dtype),
        in_specs=[far, vmem, vmem, vmem, far, far],
        out_specs=far,
        scratch_shapes=[
            pltpu.VMEM((rows, width), BF),
            pltpu.VMEM(w_up.shape, BF),
            pltpu.VMEM(w_down.shape, BF),
            pltpu.VMEM((rows * width // LANES, LANES), F32),
            pltpu.VMEM((rows * width // LANES, LANES), F32),
            pltpu.VMEM((rows, width), BF),
            pltpu.VMEM((1, rows), jnp.int32),
            pltpu.SMEM((1, rows), jnp.int32),
            dma((chunks,)),
            dma((3,)),
            dma((chunks,)),
        ],
        compiler_params=pltpu.CompilerParams(vmem_limit_bytes=VMEM_MLP),
        name="mlp",
    )(mid, coarse, ball_order, gain_mlp.reshape(1, width), w_up, w_down)


def solution(mesh):
    rows = P(("groups", "seq", "rep"))
    sizes = (mesh.shape["seq"], mesh.shape["rep"])
    return jax.shard_map(
        functools.partial(on_device, sizes),
        mesh=mesh,
        in_specs=(P(("groups", "seq", "rep"), None),) * 2 + (rows,) + (P(),) * 9,
        out_specs=P(("groups", "seq", "rep"), None),
        check_vma=False,
    )
```

```python
import functools
import math

import jax
import jax.numpy as jnp
from jax import lax
from jax.experimental import pallas as pl
from jax.experimental.pallas import tpu as pltpu
from jax.sharding import PartitionSpec as P

BALL = 128
POOL = 64
EPS = 1e-06
VMEM_ATTEND = 32 << 20
VMEM_MLP = 32 << 20
LANES = 128
GELU_A = math.sqrt(2.0 / math.pi)
GELU_B = 0.044715 * math.sqrt(2.0 / math.pi)
NO_TOKEN = 1024.0
LOG2E = 1.4426950408889634
MESH = pl.DeviceIdType.MESH
BF = jnp.bfloat16
F32 = jnp.float32


def dot(a, b):
    return jnp.dot(a, b, preferred_element_type=F32)


def dot_t(a, b):
    return lax.dot_general(a, b, (((1,), (1,)), ((), ())), preferred_element_type=F32)


def gelu_of_half(half):
    inner = half * (2.0 * GELU_A + 8.0 * GELU_B * (half * half))
    return half + half * jnp.tanh(inner)


def rms(values, gain):
    return values * lax.rsqrt(jnp.mean(values * values, axis=-1, keepdims=True) + EPS) * gain


def attend_kernel(
    sizes,
    points_hbm,
    order_hbm,
    counts_hbm,
    gain_hbm,
    temps_hbm,
    w_qkv_hbm,
    w_out_hbm,
    c_qkv_hbm,
    c_out_hbm,
    mid,
    coarse,
    points,
    order,
    order_twice,
    gain_attn,
    spots,
    counts,
    temps,
    wide,
    picked,
    srt,
    nrm,
    stage,
    tokens_all,
    w_qkv,
    w_out,
    c_qkv,
    c_out,
    points_sem,
    load_sem,
    seq_send,
    rep_send,
    recv_sem,
):
    seq_n, rep_n, heads = sizes
    peers = seq_n * rep_n
    rows, width = points.shape
    head_dim = width // heads
    chunk = 4 * BALL
    chunks = rows // chunk
    tokens = chunk // POOL
    coarse_rows = rows // POOL
    halves = width // LANES
    my_seq = lax.axis_index("seq")
    my_rep = lax.axis_index("rep")
    me = my_seq * rep_n + my_rep

    small = [
        pltpu.make_async_copy(source, target, load_sem.at[n])
        for n, (source, target) in enumerate(
            [(order_hbm, order), (counts_hbm, counts), (temps_hbm, temps), (gain_hbm, gain_attn)]
        )
    ]
    loads = [
        pltpu.make_async_copy(source, target, load_sem.at[4 + n])
        for n, (source, target) in enumerate(
            [(w_qkv_hbm, w_qkv), (w_out_hbm, w_out), (c_qkv_hbm, c_qkv), (c_out_hbm, c_out)]
        )
    ]
    load_spots = pltpu.make_async_copy(order_twice, spots, load_sem.at[8])

    def enter(i):
        spot = pl.ds(i * chunk, chunk)
        return pltpu.make_async_copy(points_hbm.at[spot, :], points.at[spot, :], points_sem.at[i])

    small[0].start()
    for i in range(chunks):
        enter(i).start()
    for load in small[1:] + loads:
        load.start()

    barrier = pltpu.get_barrier_semaphore()

    def greet_seq(step, carry):
        place = {"seq": lax.rem(my_seq + step, seq_n), "rep": my_rep}
        pl.semaphore_signal(barrier, inc=1, device_id=place, device_id_type=MESH)
        return carry

    def greet_rep(step, carry):
        place = {"seq": my_seq, "rep": lax.rem(my_rep + step, rep_n)}
        pl.semaphore_signal(barrier, inc=1, device_id=place, device_id_type=MESH)
        return carry

    lax.fori_loop(1, seq_n, greet_seq, 0)
    lax.fori_loop(1, rep_n, greet_rep, 0)

    small[0].wait()
    order_twice[...] = order[...] * 2
    load_spots.start()

    lane_head = lax.broadcasted_iota(jnp.int32, (1, width), 1) // head_dim
    near_heads = LANES // head_dim
    slabs = [slice(g * LANES, (g + 1) * LANES) for g in range(width // LANES)]
    near = lax.broadcasted_iota(jnp.int32, (1, LANES), 1) // head_dim
    head_lanes = [(near == h).astype(F32).astype(BF) for h in range(near_heads)]

    def by_head(block):
        return jnp.concatenate([block * lanes for lanes in head_lanes], axis=0)

    block_mean = jnp.where(
        lax.broadcasted_iota(jnp.int32, (width, width), 0) // head_dim
        == lax.broadcasted_iota(jnp.int32, (width, width), 1) // head_dim,
        1.0 / head_dim,
        0.0,
    ).astype(BF)

    def lane_scale(row):
        scale = jnp.zeros((1, width), F32)
        for h in range(heads):
            scale = jnp.where(lane_head == h, temps[row, h], scale)
        return scale * (LOG2E / math.sqrt(head_dim))

    def head_rms(values):
        return values * lax.rsqrt(dot((values * values).astype(BF), block_mean) + EPS)

    for i in range(chunks):
        enter(i).wait()
        block = points[pl.ds(i * chunk, chunk), :].astype(F32)
        for n in range(halves):
            wide[pl.ds(2 * i * chunk + n, chunk, stride=2), :] = block[:, slabs[n]]
    for load in small[1:]:
        load.wait()
    load_spots.wait()

    gain_a = gain_attn[...]

    def gather_chunk(i):
        for r in range(i * chunk, (i + 1) * chunk):
            picked[pl.ds(2 * r, 2), :] = wide[pl.ds(spots[0, r], 2), :]

    def pool_chunk(i):
        sorted_rows = jnp.concatenate(
            [picked[pl.ds(2 * i * chunk + n, chunk, stride=2), :] for n in range(halves)], axis=1
        )
        spot = pl.ds(i * chunk, chunk)
        srt[spot, :] = sorted_rows.astype(BF)
        normed = rms(sorted_rows, gain_a).astype(BF)
        nrm[spot, :] = normed
        shape = (2 * tokens, chunk)
        token = lax.broadcasted_iota(jnp.int32, shape, 0)
        place = lax.broadcasted_iota(jnp.int32, shape, 1)
        half = jnp.zeros(shape, jnp.int32)
        for b in range(4):
            half = jnp.where(token // 2 == b, counts[i * 4 + b], half)
        half = jnp.clip(half - POOL * (token % 2), 0, POOL)
        offset = place - token * POOL
        take = jnp.where((offset >= 0) & (offset < half), 1.0, 0.0).astype(BF)
        total = dot(take, normed)[:tokens]
        half_f = half[:tokens, :width].astype(F32)
        stage[pl.ds(i * tokens, tokens), :] = jnp.where(
            half_f > 0.0, total / jnp.maximum(half_f, 1.0), NO_TOKEN
        )

    gather_chunk(0)
    for i in range(1, chunks):
        gather_chunk(i)
        pool_chunk(i - 1)
    pool_chunk(chunks - 1)

    own_block = stage[...].astype(BF)
    tokens_all[me] = own_block

    pl.semaphore_wait(barrier, seq_n + rep_n - 2)

    def seq_place(step):
        low = my_seq < seq_n // 2
        above = seq_n - 1 - my_seq
        rising = jnp.where(step < above, seq_n - 1 - step, step - above)
        falling = jnp.where(step < my_seq, step, seq_n - 1 - step + my_seq)
        return jnp.where(low, rising, falling)

    def seq_copy(step):
        return pltpu.make_async_remote_copy(
            src_ref=tokens_all.at[me],
            dst_ref=tokens_all.at[me],
            send_sem=seq_send.at[step],
            recv_sem=recv_sem.at[me],
            device_id={"seq": seq_place(step), "rep": my_rep},
            device_id_type=MESH,
        )

    def rep_copy(block_seq, step):
        block = block_seq * rep_n + my_rep
        return pltpu.make_async_remote_copy(
            src_ref=tokens_all.at[block],
            dst_ref=tokens_all.at[block],
            send_sem=rep_send.at[block_seq, step],
            recv_sem=recv_sem.at[block],
            device_id={"seq": my_seq, "rep": lax.rem(my_rep + step, rep_n)},
            device_id_type=MESH,
        )

    def arrival(block):
        return pltpu.make_async_remote_copy(
            src_ref=tokens_all.at[block],
            dst_ref=tokens_all.at[block],
            send_sem=seq_send.at[0],
            recv_sem=recv_sem.at[block],
            device_id={"seq": lax.rem(my_seq + 1, seq_n), "rep": my_rep},
            device_id_type=MESH,
        )

    def each(count, first, act):
        def body(step, carry):
            act(step)
            return carry

        lax.fori_loop(first, count, body, 0)

    each(seq_n - 1, 0, lambda step: seq_copy(step).start())
    each(rep_n, 1, lambda step: rep_copy(my_seq, step).start())

    def relay(step):
        place = seq_place(seq_n - 2 - step)
        arrival(place * rep_n + my_rep).wait_recv()
        each(rep_n, 1, lambda away: rep_copy(place, away).start())

    for load in loads:
        load.wait()

    q_scale = lane_scale(0)

    def ball_chunk(i, carry):
        base = pl.multiple_of(i * chunk, chunk)
        spot = pl.ds(base, chunk)
        joined = dot(nrm[spot, :], w_qkv[...])
        q = (head_rms(joined[:, :width]) * q_scale).astype(BF)
        k = head_rms(joined[:, width : 2 * width]).astype(BF)
        v = joined[:, 2 * width :]
        mixes = []
        for b in range(4):
            part = slice(b * BALL, (b + 1) * BALL)
            live = lax.broadcasted_iota(jnp.int32, (BALL, width), 0) < counts[i * 4 + b]
            vb = jnp.where(live, v[part], 0.0).astype(BF)
            ones = by_head(jnp.where(live[:, :LANES], 1.0, 0.0).astype(BF))
            slab_mixes = []
            for slab in slabs:
                weights = jnp.exp2(dot_t(q[part, slab], by_head(k[part, slab]))).astype(BF)
                mixed = dot(weights, jnp.concatenate([by_head(vb[:, slab]), ones], axis=1))
                slab_mixes.append((mixed[:, :LANES] / mixed[:, LANES:]).astype(BF))
            mixes.append(jnp.concatenate(slab_mixes, axis=1))
        fine = dot(jnp.concatenate(mixes, axis=0), w_out[...])
        mid[spot, :] = (srt[spot, :].astype(F32) + fine).astype(BF)
        return carry

    def ball_step(i, carry):
        ball_chunk(i, carry)
        return carry

    early = chunks // 2
    first = (seq_n - 1) // 2
    lax.fori_loop(0, early, ball_step, 0)
    each(first, 0, relay)
    lax.fori_loop(early, chunks - 1, ball_step, 0)
    each(seq_n - 1, first, relay)
    lax.fori_loop(chunks - 1, chunks, ball_step, 0)

    own_tokens = jnp.where(own_block < NO_TOKEN / 2, own_block, 0.0).astype(BF)
    q_c = dot(own_tokens, c_qkv[:, :width])
    q_c = (head_rms(q_c) * lane_scale(1)).astype(BF)
    queries = [by_head(q_c[:, slab]) for slab in slabs]

    def gathered(step):
        def one(away):
            rep = lax.rem(my_rep + step, rep_n)
            arrival(lax.rem(my_seq + away, seq_n) * rep_n + rep).wait_recv()

        each(seq_n, 0, one)

    each(rep_n, 1, gathered)

    group = math.gcd(peers, 16)

    def coarse_keys(g):
        block = tokens_all[pl.ds(g * group, group)].reshape(group * coarse_rows, width)
        there = block < NO_TOKEN / 2
        ones = jnp.where(there[:, :LANES], 1.0, 0.0).astype(BF)
        joined = dot(jnp.where(there, block, 0.0).astype(BF), c_qkv[:, width:])
        keys = head_rms(joined[:, :width]).astype(BF)
        values = joined[:, width:].astype(BF)
        sums = []
        for query, slab in zip(queries, slabs):
            weights = jnp.exp2(dot_t(query, keys[:, slab])).astype(BF)
            sums.append(dot(weights, jnp.concatenate([values[:, slab], ones], axis=1)))
        return sums

    if peers == group:
        sums = coarse_keys(0)
    else:
        sums = lax.fori_loop(
            0,
            peers // group,
            lambda g, total: [a + b for a, b in zip(total, coarse_keys(g))],
            [jnp.zeros((near_heads * coarse_rows, 2 * LANES), F32) for _ in slabs],
        )
    slab_mixes = []
    for total in sums:
        ratio = total[:, :LANES] / total[:, LANES:]
        mix = jnp.zeros((coarse_rows, LANES), F32)
        for h in range(near_heads):
            mix = jnp.where(near == h, ratio[h * coarse_rows : (h + 1) * coarse_rows], mix)
        slab_mixes.append(mix)
    mix = jnp.concatenate(slab_mixes, axis=1)
    coarse[...] = dot(mix.astype(BF), c_out[...])

    each(seq_n - 1, 0, lambda step: seq_copy(step).wait_send())
    each(seq_n, 0, lambda away: each(rep_n, 1, lambda step: rep_copy(away, step).wait_send()))


def mlp_kernel(
    mid_hbm,
    coarse,
    order,
    gain_mlp,
    w_up_hbm,
    w_down_hbm,
    out,
    mid,
    w_up,
    w_down,
    res,
    ready,
    packed,
    order_twice,
    spots,
    mid_sem,
    load_sem,
    out_sem,
):
    rows, width = mid.shape
    chunk = 4 * BALL
    chunks = rows // chunk
    tokens = chunk // POOL
    gain_half = gain_mlp[...] * 0.5

    def enter(i):
        spot = pl.ds(i * chunk, chunk)
        return pltpu.make_async_copy(mid_hbm.at[spot, :], mid.at[spot, :], mid_sem.at[i])

    order_twice[...] = order[...] * 2
    load_up = pltpu.make_async_copy(w_up_hbm, w_up, load_sem.at[0])
    load_down = pltpu.make_async_copy(w_down_hbm, w_down, load_sem.at[1])
    load_spots = pltpu.make_async_copy(order_twice, spots, load_sem.at[2])
    enter(0).start()
    load_up.start()
    load_down.start()
    for i in range(1, chunks):
        enter(i).start()
    load_spots.start()
    load_up.wait()
    load_down.wait()

    def mlp_chunk(i):
        terms = coarse[pl.ds(i * tokens, tokens), :]
        spread = jnp.concatenate(
            [jnp.broadcast_to(terms[t : t + 1], (POOL, width)) for t in range(tokens)], axis=0
        )
        middle = mid[pl.ds(i * chunk, chunk), :].astype(F32) + spread
        mlp_in = rms(middle, gain_half).astype(BF)
        activated = gelu_of_half(dot(mlp_in, w_up[...]).astype(BF))
        result = middle + dot(activated, w_down[...])
        for n in range(width // LANES):
            res[pl.ds(2 * i * chunk + n, chunk, stride=2), :] = result[:, n * LANES : (n + 1) * LANES]

    def scatter_chunk(i):
        for r in range(i * chunk, (i + 1) * chunk):
            ready[pl.ds(spots[0, r], 2), :] = res[pl.ds(2 * r, 2), :]

    enter(0).wait()
    mlp_chunk(0)
    for i in range(1, chunks):
        enter(i).wait()
    load_spots.wait()
    for i in range(1, chunks):
        scatter_chunk(i - 1)
        mlp_chunk(i)
    scatter_chunk(chunks - 1)

    def leave(i):
        spot = pl.ds(i * chunk, chunk)
        return pltpu.make_async_copy(packed.at[spot, :], out.at[spot, :], out_sem.at[i])

    for i in range(chunks):
        packed[pl.ds(i * chunk, chunk), :] = jnp.concatenate(
            [ready[pl.ds(2 * i * chunk + n, chunk, stride=2), :] for n in range(width // LANES)], axis=1
        ).astype(BF)
        leave(i).start()
    for i in range(chunks):
        leave(i).wait()


def on_device(
    sizes,
    points,
    ball_order,
    ball_counts,
    gain_attn,
    gain_mlp,
    head_temps,
    w_qkv,
    w_out,
    c_qkv,
    c_out,
    w_up,
    w_down,
):
    rows, width = points.shape
    heads = head_temps.shape[1]
    seq_n, rep_n = sizes
    peers = seq_n * rep_n
    coarse_rows = rows // POOL
    chunks = rows // (4 * BALL)
    vmem = pl.BlockSpec(memory_space=pltpu.VMEM)
    hbm = pl.BlockSpec(memory_space=pltpu.HBM)
    far = pl.BlockSpec(memory_space=pl.ANY)
    dma = pltpu.SemaphoreType.DMA
    tall = rows * width // LANES
    mid, coarse = pl.pallas_call(
        functools.partial(attend_kernel, (*sizes, heads)),
        out_shape=(
            jax.ShapeDtypeStruct((rows, width), BF),
            jax.ShapeDtypeStruct((coarse_rows, width), F32),
        ),
        in_specs=[hbm] * 9,
        out_specs=(vmem, vmem),
        scratch_shapes=[
            pltpu.VMEM((rows, width), BF),
            pltpu.VMEM((1, rows), jnp.int32),
            pltpu.VMEM((1, rows), jnp.int32),
            pltpu.VMEM((1, width), F32),
            pltpu.SMEM((1, rows), jnp.int32),
            pltpu.SMEM(ball_counts.shape, jnp.int32),
            pltpu.SMEM(head_temps.shape, F32),
            pltpu.VMEM((tall, LANES), F32),
            pltpu.VMEM((tall, LANES), F32),
            pltpu.VMEM((rows, width), BF),
            pltpu.VMEM((rows, width), BF),
            pltpu.VMEM((coarse_rows, width), F32),
            pltpu.VMEM((peers, coarse_rows, width), BF),
            pltpu.VMEM(w_qkv.shape, BF),
            pltpu.VMEM(w_out.shape, BF),
            pltpu.VMEM(c_qkv.shape, BF),
            pltpu.VMEM(c_out.shape, BF),
            dma((chunks,)),
            dma((9,)),
            dma((seq_n,)),
            dma((seq_n, rep_n)),
            dma((peers,)),
        ],
        compiler_params=pltpu.CompilerParams(
            collective_id=0, has_side_effects=True, vmem_limit_bytes=VMEM_ATTEND
        ),
        name="attend",
    )(
        points,
        ball_order,
        ball_counts,
        gain_attn.reshape(1, width),
        head_temps,
        w_qkv,
        w_out,
        c_qkv,
        c_out,
    )
    return pl.pallas_call(
        mlp_kernel,
        out_shape=jax.ShapeDtypeStruct(points.shape, points.dtype),
        in_specs=[far, vmem, vmem, vmem, far, far],
        out_specs=far,
        scratch_shapes=[
            pltpu.VMEM((rows, width), BF),
            pltpu.VMEM(w_up.shape, BF),
            pltpu.VMEM(w_down.shape, BF),
            pltpu.VMEM((rows * width // LANES, LANES), F32),
            pltpu.VMEM((rows * width // LANES, LANES), F32),
            pltpu.VMEM((rows, width), BF),
            pltpu.VMEM((1, rows), jnp.int32),
            pltpu.SMEM((1, rows), jnp.int32),
            dma((chunks,)),
            dma((3,)),
            dma((chunks,)),
        ],
        compiler_params=pltpu.CompilerParams(vmem_limit_bytes=VMEM_MLP),
        name="mlp",
    )(mid, coarse, ball_order, gain_mlp.reshape(1, width), w_up, w_down)


def solution(mesh):
    rows = P(("groups", "seq", "rep"))
    sizes = (mesh.shape["seq"], mesh.shape["rep"])
    return jax.shard_map(
        functools.partial(on_device, sizes),
        mesh=mesh,
        in_specs=(P(("groups", "seq", "rep"), None),) * 2 + (rows,) + (P(),) * 9,
        out_specs=P(("groups", "seq", "rep"), None),
        check_vma=False,
    )
```

```python
import functools
import math

import jax
import jax.numpy as jnp
from jax import lax
from jax.experimental import pallas as pl
from jax.experimental.pallas import tpu as pltpu
from jax.sharding import PartitionSpec as P

BALL = 128
POOL = 64
EPS = 1e-06
VMEM_ATTEND = 32 << 20
VMEM_MLP = 32 << 20
LANES = 128
GELU_A = math.sqrt(2.0 / math.pi)
GELU_B = 0.044715 * math.sqrt(2.0 / math.pi)
NO_TOKEN = 1024.0
LOG2E = 1.4426950408889634
MESH = pl.DeviceIdType.MESH
BF = jnp.bfloat16
F32 = jnp.float32


def dot(a, b):
    return jnp.dot(a, b, preferred_element_type=F32)


def dot_t(a, b):
    return lax.dot_general(a, b, (((1,), (1,)), ((), ())), preferred_element_type=F32)


def gelu_of_half(half):
    inner = half * (2.0 * GELU_A + 8.0 * GELU_B * (half * half))
    return half + half * jnp.tanh(inner)


def rms(values, gain):
    return values * lax.rsqrt(jnp.mean(values * values, axis=-1, keepdims=True) + EPS) * gain


def attend_kernel(
    sizes,
    points_hbm,
    order_hbm,
    counts_hbm,
    gain_hbm,
    temps_hbm,
    w_qkv_hbm,
    w_out_hbm,
    c_qkv_hbm,
    c_out_hbm,
    gain_mlp_hbm,
    mid,
    coarse,
    gain_mid,
    points,
    order,
    order_twice,
    gain_attn,
    spots,
    counts,
    temps,
    wide,
    picked,
    srt,
    nrm,
    stage,
    tokens_all,
    w_qkv,
    w_out,
    c_qkv,
    c_out,
    points_sem,
    load_sem,
    seq_send,
    rep_send,
    recv_sem,
):
    seq_n, rep_n, heads = sizes
    peers = seq_n * rep_n
    rows, width = points.shape
    head_dim = width // heads
    chunk = 4 * BALL
    chunks = rows // chunk
    tokens = chunk // POOL
    coarse_rows = rows // POOL
    halves = width // LANES
    my_seq = lax.axis_index("seq")
    my_rep = lax.axis_index("rep")
    me = my_seq * rep_n + my_rep

    small = [
        pltpu.make_async_copy(source, target, load_sem.at[n])
        for n, (source, target) in enumerate(
            [(order_hbm, order), (counts_hbm, counts), (temps_hbm, temps), (gain_hbm, gain_attn)]
        )
    ]
    loads = [
        pltpu.make_async_copy(source, target, load_sem.at[4 + n])
        for n, (source, target) in enumerate(
            [
                (w_qkv_hbm, w_qkv),
                (w_out_hbm, w_out),
                (c_qkv_hbm, c_qkv),
                (c_out_hbm, c_out),
                (gain_mlp_hbm, gain_mid),
            ]
        )
    ]
    load_spots = pltpu.make_async_copy(order_twice, spots, load_sem.at[9])

    def enter(i):
        spot = pl.ds(i * chunk, chunk)
        return pltpu.make_async_copy(points_hbm.at[spot, :], points.at[spot, :], points_sem.at[i])

    small[0].start()
    for i in range(chunks):
        enter(i).start()
    for load in small[1:] + loads:
        load.start()

    barrier = pltpu.get_barrier_semaphore()

    def greet_seq(step, carry):
        place = {"seq": lax.rem(my_seq + step, seq_n), "rep": my_rep}
        pl.semaphore_signal(barrier, inc=1, device_id=place, device_id_type=MESH)
        return carry

    def greet_rep(step, carry):
        place = {"seq": my_seq, "rep": lax.rem(my_rep + step, rep_n)}
        pl.semaphore_signal(barrier, inc=1, device_id=place, device_id_type=MESH)
        return carry

    lax.fori_loop(1, seq_n, greet_seq, 0)
    lax.fori_loop(1, rep_n, greet_rep, 0)

    small[0].wait()
    order_twice[...] = order[...] * 2
    load_spots.start()

    lane_head = lax.broadcasted_iota(jnp.int32, (1, width), 1) // head_dim
    near_heads = LANES // head_dim
    slabs = [slice(g * LANES, (g + 1) * LANES) for g in range(width // LANES)]
    near = lax.broadcasted_iota(jnp.int32, (1, LANES), 1) // head_dim
    head_lanes = [(near == h).astype(F32).astype(BF) for h in range(near_heads)]

    def by_head(block):
        return jnp.concatenate([block * lanes for lanes in head_lanes], axis=0)

    block_mean = jnp.where(
        lax.broadcasted_iota(jnp.int32, (width, width), 0) // head_dim
        == lax.broadcasted_iota(jnp.int32, (width, width), 1) // head_dim,
        1.0 / head_dim,
        0.0,
    ).astype(BF)

    def lane_scale(row):
        scale = jnp.zeros((1, width), F32)
        for h in range(heads):
            scale = jnp.where(lane_head == h, temps[row, h], scale)
        return scale * (LOG2E / math.sqrt(head_dim))

    def head_rms(values):
        return values * lax.rsqrt(dot((values * values).astype(BF), block_mean) + EPS)

    for i in range(chunks):
        enter(i).wait()
        block = points[pl.ds(i * chunk, chunk), :].astype(F32)
        for n in range(halves):
            wide[pl.ds(2 * i * chunk + n, chunk, stride=2), :] = block[:, slabs[n]]
    for load in small[1:]:
        load.wait()
    load_spots.wait()

    gain_a = gain_attn[...]

    def gather_chunk(i):
        for r in range(i * chunk, (i + 1) * chunk):
            picked[pl.ds(2 * r, 2), :] = wide[pl.ds(spots[0, r], 2), :]

    def pool_chunk(i):
        sorted_rows = jnp.concatenate(
            [picked[pl.ds(2 * i * chunk + n, chunk, stride=2), :] for n in range(halves)], axis=1
        )
        spot = pl.ds(i * chunk, chunk)
        srt[spot, :] = sorted_rows.astype(BF)
        normed = rms(sorted_rows, gain_a).astype(BF)
        nrm[spot, :] = normed
        shape = (2 * tokens, chunk)
        token = lax.broadcasted_iota(jnp.int32, shape, 0)
        place = lax.broadcasted_iota(jnp.int32, shape, 1)
        half = jnp.zeros(shape, jnp.int32)
        for b in range(4):
            half = jnp.where(token // 2 == b, counts[i * 4 + b], half)
        half = jnp.clip(half - POOL * (token % 2), 0, POOL)
        offset = place - token * POOL
        take = jnp.where((offset >= 0) & (offset < half), 1.0, 0.0).astype(BF)
        total = dot(take, normed)[:tokens]
        half_f = half[:tokens, :width].astype(F32)
        stage[pl.ds(i * tokens, tokens), :] = jnp.where(
            half_f > 0.0, total / jnp.maximum(half_f, 1.0), NO_TOKEN
        )

    gather_chunk(0)
    for i in range(1, chunks):
        gather_chunk(i)
        pool_chunk(i - 1)
    pool_chunk(chunks - 1)

    own_block = stage[...].astype(BF)
    tokens_all[me] = own_block

    pl.semaphore_wait(barrier, seq_n + rep_n - 2)

    def seq_place(step):
        low = my_seq < seq_n // 2
        above = seq_n - 1 - my_seq
        rising = jnp.where(step < above, seq_n - 1 - step, step - above)
        falling = jnp.where(step < my_seq, step, seq_n - 1 - step + my_seq)
        return jnp.where(low, rising, falling)

    def seq_copy(step):
        return pltpu.make_async_remote_copy(
            src_ref=tokens_all.at[me],
            dst_ref=tokens_all.at[me],
            send_sem=seq_send.at[step],
            recv_sem=recv_sem.at[me],
            device_id={"seq": seq_place(step), "rep": my_rep},
            device_id_type=MESH,
        )

    def rep_copy(block_seq, step):
        block = block_seq * rep_n + my_rep
        return pltpu.make_async_remote_copy(
            src_ref=tokens_all.at[block],
            dst_ref=tokens_all.at[block],
            send_sem=rep_send.at[block_seq, step],
            recv_sem=recv_sem.at[block],
            device_id={"seq": my_seq, "rep": lax.rem(my_rep + step, rep_n)},
            device_id_type=MESH,
        )

    def arrival(block):
        return pltpu.make_async_remote_copy(
            src_ref=tokens_all.at[block],
            dst_ref=tokens_all.at[block],
            send_sem=seq_send.at[0],
            recv_sem=recv_sem.at[block],
            device_id={"seq": lax.rem(my_seq + 1, seq_n), "rep": my_rep},
            device_id_type=MESH,
        )

    def each(count, first, act):
        def body(step, carry):
            act(step)
            return carry

        lax.fori_loop(first, count, body, 0)

    each(seq_n - 1, 0, lambda step: seq_copy(step).start())
    each(rep_n, 1, lambda step: rep_copy(my_seq, step).start())

    def relay(step):
        place = seq_place(seq_n - 2 - step)
        arrival(place * rep_n + my_rep).wait_recv()
        each(rep_n, 1, lambda away: rep_copy(place, away).start())

    for load in loads:
        load.wait()

    q_scale = lane_scale(0)

    def ball_chunk(i, carry):
        base = pl.multiple_of(i * chunk, chunk)
        spot = pl.ds(base, chunk)
        joined = dot(nrm[spot, :], w_qkv[...])
        q = (head_rms(joined[:, :width]) * q_scale).astype(BF)
        k = head_rms(joined[:, width : 2 * width]).astype(BF)
        v = joined[:, 2 * width :]
        mixes = []
        for b in range(4):
            part = slice(b * BALL, (b + 1) * BALL)
            live = lax.broadcasted_iota(jnp.int32, (BALL, width), 0) < counts[i * 4 + b]
            vb = jnp.where(live, v[part], 0.0).astype(BF)
            ones = by_head(jnp.where(live[:, :LANES], 1.0, 0.0).astype(BF))
            slab_mixes = []
            for slab in slabs:
                weights = jnp.exp2(dot_t(q[part, slab], by_head(k[part, slab]))).astype(BF)
                mixed = dot(weights, jnp.concatenate([by_head(vb[:, slab]), ones], axis=1))
                slab_mixes.append((mixed[:, :LANES] / mixed[:, LANES:]).astype(BF))
            mixes.append(jnp.concatenate(slab_mixes, axis=1))
        fine = dot(jnp.concatenate(mixes, axis=0), w_out[...])
        mid[spot, :] = (srt[spot, :].astype(F32) + fine).astype(BF)
        return carry

    def ball_step(i, carry):
        ball_chunk(i, carry)
        return carry

    early = chunks // 2
    first = (seq_n - 1) // 2
    lax.fori_loop(0, early, ball_step, 0)
    each(first, 0, relay)
    lax.fori_loop(early, chunks - 1, ball_step, 0)
    each(seq_n - 1, first, relay)
    lax.fori_loop(chunks - 1, chunks, ball_step, 0)

    own_tokens = jnp.where(own_block < NO_TOKEN / 2, own_block, 0.0).astype(BF)
    q_c = dot(own_tokens, c_qkv[:, :width])
    q_c = (head_rms(q_c) * lane_scale(1)).astype(BF)
    queries = [by_head(q_c[:, slab]) for slab in slabs]

    def gathered(step):
        def one(away):
            rep = lax.rem(my_rep + step, rep_n)
            arrival(lax.rem(my_seq + away, seq_n) * rep_n + rep).wait_recv()

        each(seq_n, 0, one)

    each(rep_n, 1, gathered)

    group = math.gcd(peers, 16)

    def coarse_keys(g):
        block = tokens_all[pl.ds(g * group, group)].reshape(group * coarse_rows, width)
        there = block < NO_TOKEN / 2
        ones = jnp.where(there[:, :LANES], 1.0, 0.0).astype(BF)
        joined = dot(jnp.where(there, block, 0.0).astype(BF), c_qkv[:, width:])
        keys = head_rms(joined[:, :width]).astype(BF)
        values = joined[:, width:].astype(BF)
        sums = []
        for query, slab in zip(queries, slabs):
            weights = jnp.exp2(dot_t(query, keys[:, slab])).astype(BF)
            sums.append(dot(weights, jnp.concatenate([values[:, slab], ones], axis=1)))
        return sums

    if peers == group:
        sums = coarse_keys(0)
    else:
        sums = lax.fori_loop(
            0,
            peers // group,
            lambda g, total: [a + b for a, b in zip(total, coarse_keys(g))],
            [jnp.zeros((near_heads * coarse_rows, 2 * LANES), F32) for _ in slabs],
        )
    slab_mixes = []
    for total in sums:
        ratio = total[:, :LANES] / total[:, LANES:]
        mix = jnp.zeros((coarse_rows, LANES), F32)
        for h in range(near_heads):
            mix = jnp.where(near == h, ratio[h * coarse_rows : (h + 1) * coarse_rows], mix)
        slab_mixes.append(mix)
    mix = jnp.concatenate(slab_mixes, axis=1)
    coarse[...] = dot(mix.astype(BF), c_out[...])

    each(seq_n - 1, 0, lambda step: seq_copy(step).wait_send())
    each(seq_n, 0, lambda away: each(rep_n, 1, lambda step: rep_copy(away, step).wait_send()))


def mlp_kernel(
    mid,
    coarse,
    order,
    gain_mlp,
    w_up,
    w_down,
    out,
    res,
    ready,
    packed,
    order_twice,
    spots,
    load_sem,
    out_sem,
):
    rows, width = mid.shape
    chunk = 4 * BALL
    chunks = rows // chunk
    tokens = chunk // POOL
    gain_half = gain_mlp[...] * 0.5

    order_twice[...] = order[...] * 2
    load_spots = pltpu.make_async_copy(order_twice, spots, load_sem)
    load_spots.start()

    def mlp_chunk(i):
        terms = coarse[pl.ds(i * tokens, tokens), :]
        spread = jnp.concatenate(
            [jnp.broadcast_to(terms[t : t + 1], (POOL, width)) for t in range(tokens)], axis=0
        )
        middle = mid[pl.ds(i * chunk, chunk), :].astype(F32) + spread
        mlp_in = rms(middle, gain_half).astype(BF)
        activated = gelu_of_half(dot(mlp_in, w_up[...]).astype(BF))
        result = middle + dot(activated, w_down[...])
        for n in range(width // LANES):
            res[pl.ds(2 * i * chunk + n, chunk, stride=2), :] = result[:, n * LANES : (n + 1) * LANES]

    def scatter_chunk(i):
        for r in range(i * chunk, (i + 1) * chunk):
            ready[pl.ds(spots[0, r], 2), :] = res[pl.ds(2 * r, 2), :]

    mlp_chunk(0)
    load_spots.wait()
    for i in range(1, chunks):
        scatter_chunk(i - 1)
        mlp_chunk(i)
    scatter_chunk(chunks - 1)

    def leave(i):
        spot = pl.ds(i * chunk, chunk)
        return pltpu.make_async_copy(packed.at[spot, :], out.at[spot, :], out_sem.at[i])

    for i in range(chunks):
        packed[pl.ds(i * chunk, chunk), :] = jnp.concatenate(
            [ready[pl.ds(2 * i * chunk + n, chunk, stride=2), :] for n in range(width // LANES)], axis=1
        ).astype(BF)
        leave(i).start()
    for i in range(chunks):
        leave(i).wait()


def on_device(
    sizes,
    points,
    ball_order,
    ball_counts,
    gain_attn,
    gain_mlp,
    head_temps,
    w_qkv,
    w_out,
    c_qkv,
    c_out,
    w_up,
    w_down,
):
    rows, width = points.shape
    heads = head_temps.shape[1]
    seq_n, rep_n = sizes
    peers = seq_n * rep_n
    coarse_rows = rows // POOL
    chunks = rows // (4 * BALL)
    vmem = pl.BlockSpec(memory_space=pltpu.VMEM)
    hbm = pl.BlockSpec(memory_space=pltpu.HBM)
    far = pl.BlockSpec(memory_space=pl.ANY)
    dma = pltpu.SemaphoreType.DMA
    tall = rows * width // LANES
    mid, coarse, gain_mid = pl.pallas_call(
        functools.partial(attend_kernel, (*sizes, heads)),
        out_shape=(
            jax.ShapeDtypeStruct((rows, width), BF),
            jax.ShapeDtypeStruct((coarse_rows, width), F32),
            jax.ShapeDtypeStruct((1, width), F32),
        ),
        in_specs=[hbm] * 10,
        out_specs=(vmem,) * 3,
        scratch_shapes=[
            pltpu.VMEM((rows, width), BF),
            pltpu.VMEM((1, rows), jnp.int32),
            pltpu.VMEM((1, rows), jnp.int32),
            pltpu.VMEM((1, width), F32),
            pltpu.SMEM((1, rows), jnp.int32),
            pltpu.SMEM(ball_counts.shape, jnp.int32),
            pltpu.SMEM(head_temps.shape, F32),
            pltpu.VMEM((tall, LANES), F32),
            pltpu.VMEM((tall, LANES), F32),
            pltpu.VMEM((rows, width), BF),
            pltpu.VMEM((rows, width), BF),
            pltpu.VMEM((coarse_rows, width), F32),
            pltpu.VMEM((peers, coarse_rows, width), BF),
            pltpu.VMEM(w_qkv.shape, BF),
            pltpu.VMEM(w_out.shape, BF),
            pltpu.VMEM(c_qkv.shape, BF),
            pltpu.VMEM(c_out.shape, BF),
            dma((chunks,)),
            dma((10,)),
            dma((seq_n,)),
            dma((seq_n, rep_n)),
            dma((peers,)),
        ],
        compiler_params=pltpu.CompilerParams(
            collective_id=0, has_side_effects=True, vmem_limit_bytes=VMEM_ATTEND
        ),
        name="attend",
    )(
        *(
            pltpu.with_memory_space_constraint(operand, pltpu.HBM)
            for operand in (
                points,
                ball_order,
                ball_counts,
                gain_attn.reshape(1, width),
                head_temps,
                w_qkv,
                w_out,
                c_qkv,
                c_out,
                gain_mlp.reshape(1, width),
            )
        )
    )
    return pl.pallas_call(
        mlp_kernel,
        out_shape=jax.ShapeDtypeStruct(points.shape, points.dtype),
        in_specs=[vmem] * 6,
        out_specs=far,
        scratch_shapes=[
            pltpu.VMEM((tall, LANES), F32),
            pltpu.VMEM((tall, LANES), F32),
            pltpu.VMEM((rows, width), BF),
            pltpu.VMEM((1, rows), jnp.int32),
            pltpu.SMEM((1, rows), jnp.int32),
            dma,
            dma((chunks,)),
        ],
        compiler_params=pltpu.CompilerParams(vmem_limit_bytes=VMEM_MLP),
        name="mlp",
    )(mid, coarse, ball_order, gain_mid, w_up, w_down)


def solution(mesh):
    rows = P(("groups", "seq", "rep"))
    sizes = (mesh.shape["seq"], mesh.shape["rep"])
    return jax.shard_map(
        functools.partial(on_device, sizes),
        mesh=mesh,
        in_specs=(P(("groups", "seq", "rep"), None),) * 2 + (rows,) + (P(),) * 9,
        out_specs=P(("groups", "seq", "rep"), None),
        check_vma=False,
    )
```

```python
import functools
import math

import jax
import jax.numpy as jnp
from jax import lax
from jax.experimental import pallas as pl
from jax.experimental.pallas import tpu as pltpu
from jax.sharding import PartitionSpec as P

BALL = 128
POOL = 64
EPS = 1e-06
VMEM_ATTEND = 32 << 20
VMEM_MLP = 32 << 20
LANES = 128
GELU_A = math.sqrt(2.0 / math.pi)
GELU_B = 0.044715 * math.sqrt(2.0 / math.pi)
NO_TOKEN = 1024.0
LOG2E = 1.4426950408889634
MESH = pl.DeviceIdType.MESH
BF = jnp.bfloat16
F32 = jnp.float32


def dot(a, b):
    return jnp.dot(a, b, preferred_element_type=F32)


def dot_t(a, b):
    return lax.dot_general(a, b, (((1,), (1,)), ((), ())), preferred_element_type=F32)


def gelu_of_half(half):
    inner = half * (2.0 * GELU_A + 8.0 * GELU_B * (half * half))
    return half + half * jnp.tanh(inner)


def rms(values, gain):
    return values * lax.rsqrt(jnp.mean(values * values, axis=-1, keepdims=True) + EPS) * gain


def attend_kernel(
    sizes,
    points_hbm,
    order_hbm,
    counts_hbm,
    gain_hbm,
    temps_hbm,
    w_qkv_hbm,
    w_out_hbm,
    c_qkv_hbm,
    c_out_hbm,
    gain_mlp_hbm,
    mid,
    coarse,
    gain_mid,
    points,
    order,
    order_twice,
    gain_attn,
    spots,
    counts,
    temps,
    wide,
    picked,
    srt,
    nrm,
    stage,
    tokens_all,
    w_qkv,
    w_out,
    c_qkv,
    c_out,
    points_sem,
    load_sem,
    direct_send,
    pair_send,
    recv_sem,
):
    seq_n, rep_n, heads = sizes
    peers = seq_n * rep_n
    rows, width = points.shape
    head_dim = width // heads
    chunk = 4 * BALL
    chunks = rows // chunk
    tokens = chunk // POOL
    coarse_rows = rows // POOL
    halves = width // LANES
    my_seq = lax.axis_index("seq")
    my_rep = lax.axis_index("rep")
    me = my_seq * rep_n + my_rep
    pair = 2 if rep_n % 2 == 0 else 1
    pairs = rep_n // pair
    direct = seq_n * pairs - 1

    small = [
        pltpu.make_async_copy(source, target, load_sem.at[n])
        for n, (source, target) in enumerate(
            [(order_hbm, order), (counts_hbm, counts), (temps_hbm, temps), (gain_hbm, gain_attn)]
        )
    ]
    loads = [
        pltpu.make_async_copy(source, target, load_sem.at[4 + n])
        for n, (source, target) in enumerate(
            [
                (w_qkv_hbm, w_qkv),
                (w_out_hbm, w_out),
                (c_qkv_hbm, c_qkv),
                (c_out_hbm, c_out),
                (gain_mlp_hbm, gain_mid),
            ]
        )
    ]
    load_spots = pltpu.make_async_copy(order_twice, spots, load_sem.at[9])

    def enter(i):
        spot = pl.ds(i * chunk, chunk)
        return pltpu.make_async_copy(points_hbm.at[spot, :], points.at[spot, :], points_sem.at[i])

    small[0].start()
    for i in range(chunks):
        enter(i).start()
    for load in small[1:] + loads:
        load.start()

    barrier = pltpu.get_barrier_semaphore()

    def each(count, first, act):
        def body(step, carry):
            act(step)
            return carry

        lax.fori_loop(first, count, body, 0)

    def seq_place(step):
        above = seq_n - 1 - my_seq
        rising = jnp.where(step < above, seq_n - 1 - step, step - above)
        falling = jnp.where(step < my_seq, step, seq_n - 1 - step + my_seq)
        return jnp.where(my_seq < seq_n // 2, rising, falling)

    def place_of(step):
        away = step // pairs
        seq = jnp.where(away < seq_n - 1, seq_place(away), my_seq)
        rep = lax.rem(my_rep + pair * (1 + lax.rem(step, pairs)), rep_n)
        return seq, rep

    def partner_of(step):
        return my_rep - lax.rem(my_rep, pair) + lax.rem(my_rep + step, pair)

    def greet(seq, rep):
        pl.semaphore_signal(
            barrier, inc=1, device_id={"seq": seq, "rep": rep}, device_id_type=MESH
        )

    each(direct, 0, lambda step: greet(*place_of(step)))
    each(pair, 1, lambda step: greet(my_seq, partner_of(step)))

    small[0].wait()
    order_twice[...] = order[...] * 2
    load_spots.start()

    lane_head = lax.broadcasted_iota(jnp.int32, (1, width), 1) // head_dim
    near_heads = LANES // head_dim
    slabs = [slice(g * LANES, (g + 1) * LANES) for g in range(width // LANES)]
    near = lax.broadcasted_iota(jnp.int32, (1, LANES), 1) // head_dim
    head_lanes = [(near == h).astype(F32).astype(BF) for h in range(near_heads)]

    def by_head(block):
        return jnp.concatenate([block * lanes for lanes in head_lanes], axis=0)

    block_mean = jnp.where(
        lax.broadcasted_iota(jnp.int32, (width, width), 0) // head_dim
        == lax.broadcasted_iota(jnp.int32, (width, width), 1) // head_dim,
        1.0 / head_dim,
        0.0,
    ).astype(BF)

    def lane_scale(row):
        scale = jnp.zeros((1, width), F32)
        for h in range(heads):
            scale = jnp.where(lane_head == h, temps[row, h], scale)
        return scale * (LOG2E / math.sqrt(head_dim))

    def head_rms(values):
        return values * lax.rsqrt(dot((values * values).astype(BF), block_mean) + EPS)

    for i in range(chunks):
        enter(i).wait()
        block = points[pl.ds(i * chunk, chunk), :].astype(F32)
        for n in range(halves):
            wide[pl.ds(2 * i * chunk + n, chunk, stride=2), :] = block[:, slabs[n]]
    for load in small[1:]:
        load.wait()
    load_spots.wait()

    gain_a = gain_attn[...]

    def gather_chunk(i):
        for r in range(i * chunk, (i + 1) * chunk):
            picked[pl.ds(2 * r, 2), :] = wide[pl.ds(spots[0, r], 2), :]

    def pool_chunk(i):
        sorted_rows = jnp.concatenate(
            [picked[pl.ds(2 * i * chunk + n, chunk, stride=2), :] for n in range(halves)], axis=1
        )
        spot = pl.ds(i * chunk, chunk)
        srt[spot, :] = sorted_rows.astype(BF)
        normed = rms(sorted_rows, gain_a).astype(BF)
        nrm[spot, :] = normed
        shape = (2 * tokens, chunk)
        token = lax.broadcasted_iota(jnp.int32, shape, 0)
        place = lax.broadcasted_iota(jnp.int32, shape, 1)
        half = jnp.zeros(shape, jnp.int32)
        for b in range(4):
            half = jnp.where(token // 2 == b, counts[i * 4 + b], half)
        half = jnp.clip(half - POOL * (token % 2), 0, POOL)
        offset = place - token * POOL
        take = jnp.where((offset >= 0) & (offset < half), 1.0, 0.0).astype(BF)
        total = dot(take, normed)[:tokens]
        half_f = half[:tokens, :width].astype(F32)
        stage[pl.ds(i * tokens, tokens), :] = jnp.where(
            half_f > 0.0, total / jnp.maximum(half_f, 1.0), NO_TOKEN
        )

    gather_chunk(0)
    for i in range(1, chunks):
        gather_chunk(i)
        pool_chunk(i - 1)
    pool_chunk(chunks - 1)

    own_block = stage[...].astype(BF)
    tokens_all[me] = own_block

    pl.semaphore_wait(barrier, direct + pair - 1)

    def copy_of(block, send_sem, seq, rep):
        return pltpu.make_async_remote_copy(
            src_ref=tokens_all.at[block],
            dst_ref=tokens_all.at[block],
            send_sem=send_sem,
            recv_sem=recv_sem.at[block],
            device_id={"seq": seq, "rep": rep},
            device_id_type=MESH,
        )

    def spread(step):
        return copy_of(me, direct_send.at[step], *place_of(step))

    def forward(block, step):
        return copy_of(block, pair_send.at[block, step], my_seq, partner_of(step))

    def arrival(block):
        return copy_of(block, direct_send.at[0], *place_of(0))

    each(direct, 0, lambda step: spread(step).start())
    each(pair, 1, lambda step: forward(me, step).start())

    def block_of(step):
        seq, rep = place_of(direct - 1 - step)
        return seq * rep_n + rep

    def relay(step):
        block = block_of(step)
        arrival(block).wait_recv()
        each(pair, 1, lambda away: forward(block, away).start())

    for load in loads:
        load.wait()

    q_scale = lane_scale(0)

    def ball_chunk(i, carry):
        base = pl.multiple_of(i * chunk, chunk)
        spot = pl.ds(base, chunk)
        joined = dot(nrm[spot, :], w_qkv[...])
        q = (head_rms(joined[:, :width]) * q_scale).astype(BF)
        k = head_rms(joined[:, width : 2 * width]).astype(BF)
        v = joined[:, 2 * width :]
        mixes = []
        for b in range(4):
            part = slice(b * BALL, (b + 1) * BALL)
            live = lax.broadcasted_iota(jnp.int32, (BALL, width), 0) < counts[i * 4 + b]
            vb = jnp.where(live, v[part], 0.0).astype(BF)
            ones = by_head(jnp.where(live[:, :LANES], 1.0, 0.0).astype(BF))
            slab_mixes = []
            for slab in slabs:
                weights = jnp.exp2(dot_t(q[part, slab], by_head(k[part, slab]))).astype(BF)
                mixed = dot(weights, jnp.concatenate([by_head(vb[:, slab]), ones], axis=1))
                slab_mixes.append((mixed[:, :LANES] / mixed[:, LANES:]).astype(BF))
            mixes.append(jnp.concatenate(slab_mixes, axis=1))
        fine = dot(jnp.concatenate(mixes, axis=0), w_out[...])
        mid[spot, :] = (srt[spot, :].astype(F32) + fine).astype(BF)
        return carry

    def ball_step(i, carry):
        ball_chunk(i, carry)
        return carry

    early = chunks // 2
    first = direct // 2
    lax.fori_loop(0, early, ball_step, 0)
    each(first, 0, relay)
    lax.fori_loop(early, chunks - 1, ball_step, 0)
    each(direct, first, relay)
    lax.fori_loop(chunks - 1, chunks, ball_step, 0)

    own_tokens = jnp.where(own_block < NO_TOKEN / 2, own_block, 0.0).astype(BF)
    q_c = dot(own_tokens, c_qkv[:, :width])
    q_c = (head_rms(q_c) * lane_scale(1)).astype(BF)
    queries = [by_head(q_c[:, slab]) for slab in slabs]

    def gathered(step):
        rep = partner_of(step)
        each(pairs, 0, lambda away: each(seq_n, 0, lambda seq: arrival(
            seq * rep_n + lax.rem(rep + pair * away, rep_n)
        ).wait_recv()))

    each(pair, 1, gathered)

    group = math.gcd(peers, 16)

    def coarse_keys(g):
        block = tokens_all[pl.ds(g * group, group)].reshape(group * coarse_rows, width)
        there = block < NO_TOKEN / 2
        ones = jnp.where(there[:, :LANES], 1.0, 0.0).astype(BF)
        joined = dot(jnp.where(there, block, 0.0).astype(BF), c_qkv[:, width:])
        keys = head_rms(joined[:, :width]).astype(BF)
        values = joined[:, width:].astype(BF)
        sums = []
        for query, slab in zip(queries, slabs):
            weights = jnp.exp2(dot_t(query, keys[:, slab])).astype(BF)
            sums.append(dot(weights, jnp.concatenate([values[:, slab], ones], axis=1)))
        return sums

    if peers == group:
        sums = coarse_keys(0)
    else:
        sums = lax.fori_loop(
            0,
            peers // group,
            lambda g, total: [a + b for a, b in zip(total, coarse_keys(g))],
            [jnp.zeros((near_heads * coarse_rows, 2 * LANES), F32) for _ in slabs],
        )
    slab_mixes = []
    for total in sums:
        ratio = total[:, :LANES] / total[:, LANES:]
        mix = jnp.zeros((coarse_rows, LANES), F32)
        for h in range(near_heads):
            mix = jnp.where(near == h, ratio[h * coarse_rows : (h + 1) * coarse_rows], mix)
        slab_mixes.append(mix)
    mix = jnp.concatenate(slab_mixes, axis=1)
    coarse[...] = dot(mix.astype(BF), c_out[...])

    each(direct, 0, lambda step: spread(step).wait_send())
    each(pair, 1, lambda step: forward(me, step).wait_send())
    each(direct, 0, lambda step: each(
        pair, 1, lambda away: forward(block_of(step), away).wait_send()
    ))


def mlp_kernel(
    mid,
    coarse,
    order,
    gain_mlp,
    w_up,
    w_down,
    out,
    res,
    ready,
    packed,
    order_twice,
    spots,
    load_sem,
    out_sem,
):
    rows, width = mid.shape
    chunk = 4 * BALL
    chunks = rows // chunk
    tokens = chunk // POOL
    gain_half = gain_mlp[...] * 0.5

    order_twice[...] = order[...] * 2
    load_spots = pltpu.make_async_copy(order_twice, spots, load_sem)
    load_spots.start()

    def mlp_chunk(i):
        terms = coarse[pl.ds(i * tokens, tokens), :]
        spread = jnp.concatenate(
            [jnp.broadcast_to(terms[t : t + 1], (POOL, width)) for t in range(tokens)], axis=0
        )
        middle = mid[pl.ds(i * chunk, chunk), :].astype(F32) + spread
        mlp_in = rms(middle, gain_half).astype(BF)
        activated = gelu_of_half(dot(mlp_in, w_up[...]).astype(BF))
        result = middle + dot(activated, w_down[...])
        for n in range(width // LANES):
            res[pl.ds(2 * i * chunk + n, chunk, stride=2), :] = result[:, n * LANES : (n + 1) * LANES]

    def scatter_chunk(i):
        for r in range(i * chunk, (i + 1) * chunk):
            ready[pl.ds(spots[0, r], 2), :] = res[pl.ds(2 * r, 2), :]

    mlp_chunk(0)
    load_spots.wait()
    for i in range(1, chunks):
        scatter_chunk(i - 1)
        mlp_chunk(i)
    scatter_chunk(chunks - 1)

    def leave(i):
        spot = pl.ds(i * chunk, chunk)
        return pltpu.make_async_copy(packed.at[spot, :], out.at[spot, :], out_sem.at[i])

    for i in range(chunks):
        packed[pl.ds(i * chunk, chunk), :] = jnp.concatenate(
            [ready[pl.ds(2 * i * chunk + n, chunk, stride=2), :] for n in range(width // LANES)], axis=1
        ).astype(BF)
        leave(i).start()
    for i in range(chunks):
        leave(i).wait()


def on_device(
    sizes,
    points,
    ball_order,
    ball_counts,
    gain_attn,
    gain_mlp,
    head_temps,
    w_qkv,
    w_out,
    c_qkv,
    c_out,
    w_up,
    w_down,
):
    rows, width = points.shape
    heads = head_temps.shape[1]
    seq_n, rep_n = sizes
    peers = seq_n * rep_n
    coarse_rows = rows // POOL
    chunks = rows // (4 * BALL)
    vmem = pl.BlockSpec(memory_space=pltpu.VMEM)
    hbm = pl.BlockSpec(memory_space=pltpu.HBM)
    far = pl.BlockSpec(memory_space=pl.ANY)
    dma = pltpu.SemaphoreType.DMA
    tall = rows * width // LANES
    mid, coarse, gain_mid = pl.pallas_call(
        functools.partial(attend_kernel, (*sizes, heads)),
        out_shape=(
            jax.ShapeDtypeStruct((rows, width), BF),
            jax.ShapeDtypeStruct((coarse_rows, width), F32),
            jax.ShapeDtypeStruct((1, width), F32),
        ),
        in_specs=[hbm] * 10,
        out_specs=(vmem,) * 3,
        scratch_shapes=[
            pltpu.VMEM((rows, width), BF),
            pltpu.VMEM((1, rows), jnp.int32),
            pltpu.VMEM((1, rows), jnp.int32),
            pltpu.VMEM((1, width), F32),
            pltpu.SMEM((1, rows), jnp.int32),
            pltpu.SMEM(ball_counts.shape, jnp.int32),
            pltpu.SMEM(head_temps.shape, F32),
            pltpu.VMEM((tall, LANES), F32),
            pltpu.VMEM((tall, LANES), F32),
            pltpu.VMEM((rows, width), BF),
            pltpu.VMEM((rows, width), BF),
            pltpu.VMEM((coarse_rows, width), F32),
            pltpu.VMEM((peers, coarse_rows, width), BF),
            pltpu.VMEM(w_qkv.shape, BF),
            pltpu.VMEM(w_out.shape, BF),
            pltpu.VMEM(c_qkv.shape, BF),
            pltpu.VMEM(c_out.shape, BF),
            dma((chunks,)),
            dma((10,)),
            dma((peers,)),
            dma((peers, 2)),
            dma((peers,)),
        ],
        compiler_params=pltpu.CompilerParams(
            collective_id=0, has_side_effects=True, vmem_limit_bytes=VMEM_ATTEND
        ),
        name="attend",
    )(
        *(
            pltpu.with_memory_space_constraint(operand, pltpu.HBM)
            for operand in (
                points,
                ball_order,
                ball_counts,
                gain_attn.reshape(1, width),
                head_temps,
                w_qkv,
                w_out,
                c_qkv,
                c_out,
                gain_mlp.reshape(1, width),
            )
        )
    )
    return pl.pallas_call(
        mlp_kernel,
        out_shape=jax.ShapeDtypeStruct(points.shape, points.dtype),
        in_specs=[vmem] * 6,
        out_specs=far,
        scratch_shapes=[
            pltpu.VMEM((tall, LANES), F32),
            pltpu.VMEM((tall, LANES), F32),
            pltpu.VMEM((rows, width), BF),
            pltpu.VMEM((1, rows), jnp.int32),
            pltpu.SMEM((1, rows), jnp.int32),
            dma,
            dma((chunks,)),
        ],
        compiler_params=pltpu.CompilerParams(vmem_limit_bytes=VMEM_MLP),
        name="mlp",
    )(mid, coarse, ball_order, gain_mid, w_up, w_down)


def solution(mesh):
    rows = P(("groups", "seq", "rep"))
    sizes = (mesh.shape["seq"], mesh.shape["rep"])
    return jax.shard_map(
        functools.partial(on_device, sizes),
        mesh=mesh,
        in_specs=(P(("groups", "seq", "rep"), None),) * 2 + (rows,) + (P(),) * 9,
        out_specs=P(("groups", "seq", "rep"), None),
        check_vma=False,
    )
```

```python
import functools
import math

import jax
import jax.numpy as jnp
from jax import lax
from jax.experimental import pallas as pl
from jax.experimental.pallas import tpu as pltpu
from jax.sharding import PartitionSpec as P

BALL = 128
POOL = 64
EPS = 1e-06
VMEM_ATTEND = 32 << 20
VMEM_MLP = 32 << 20
LANES = 128
GELU_A = math.sqrt(2.0 / math.pi)
GELU_B = 0.044715 * math.sqrt(2.0 / math.pi)
NO_TOKEN = 1024.0
LOG2E = 1.4426950408889634
MESH = pl.DeviceIdType.MESH
BF = jnp.bfloat16
F32 = jnp.float32


def dot(a, b):
    return jnp.dot(a, b, preferred_element_type=F32)


def dot_t(a, b):
    return lax.dot_general(a, b, (((1,), (1,)), ((), ())), preferred_element_type=F32)


def gelu_of_half(half):
    inner = half * (2.0 * GELU_A + 8.0 * GELU_B * (half * half))
    return half + half * jnp.tanh(inner)


def rms(values, gain):
    return values * lax.rsqrt(jnp.mean(values * values, axis=-1, keepdims=True) + EPS) * gain


def attend_kernel(
    sizes,
    points_hbm,
    order_hbm,
    counts_hbm,
    gain_hbm,
    temps_hbm,
    w_qkv_hbm,
    w_out_hbm,
    c_qkv_hbm,
    c_out_hbm,
    gain_mlp_hbm,
    mid,
    coarse,
    gain_mid,
    points,
    order,
    order_twice,
    gain_attn,
    spots,
    counts,
    temps,
    wide,
    picked,
    srt,
    nrm,
    queries,
    keys,
    values,
    stage,
    tokens_all,
    w_qkv,
    w_out,
    c_qkv,
    c_out,
    points_sem,
    load_sem,
    direct_send,
    pair_send,
    recv_sem,
):
    seq_n, rep_n, heads = sizes
    peers = seq_n * rep_n
    rows, width = points.shape
    head_dim = width // heads
    chunk = 4 * BALL
    chunks = rows // chunk
    tokens = chunk // POOL
    coarse_rows = rows // POOL
    halves = width // LANES
    my_seq = lax.axis_index("seq")
    my_rep = lax.axis_index("rep")
    me = my_seq * rep_n + my_rep
    pair = 2 if rep_n % 2 == 0 else 1
    pairs = rep_n // pair
    direct = seq_n * pairs - 1

    small = [
        pltpu.make_async_copy(source, target, load_sem.at[n])
        for n, (source, target) in enumerate(
            [(order_hbm, order), (counts_hbm, counts), (temps_hbm, temps), (gain_hbm, gain_attn)]
        )
    ]
    loads = [
        pltpu.make_async_copy(source, target, load_sem.at[4 + n])
        for n, (source, target) in enumerate(
            [
                (w_qkv_hbm, w_qkv),
                (w_out_hbm, w_out),
                (c_qkv_hbm, c_qkv),
                (c_out_hbm, c_out),
                (gain_mlp_hbm, gain_mid),
            ]
        )
    ]
    load_spots = pltpu.make_async_copy(order_twice, spots, load_sem.at[9])

    def enter(i):
        spot = pl.ds(i * chunk, chunk)
        return pltpu.make_async_copy(points_hbm.at[spot, :], points.at[spot, :], points_sem.at[i])

    small[0].start()
    for i in range(chunks):
        enter(i).start()
    for load in small[1:] + loads:
        load.start()

    barrier = pltpu.get_barrier_semaphore()

    def each(count, first, act):
        def body(step, carry):
            act(step)
            return carry

        lax.fori_loop(first, count, body, 0)

    def seq_place(step):
        above = seq_n - 1 - my_seq
        rising = jnp.where(step < above, seq_n - 1 - step, step - above)
        falling = jnp.where(step < my_seq, step, seq_n - 1 - step + my_seq)
        return jnp.where(my_seq < seq_n // 2, rising, falling)

    def place_of(step):
        away = step // pairs
        seq = jnp.where(away < seq_n - 1, seq_place(away), my_seq)
        rep = lax.rem(my_rep + pair * (1 + lax.rem(step, pairs)), rep_n)
        return seq, rep

    def partner_of(step):
        return my_rep - lax.rem(my_rep, pair) + lax.rem(my_rep + step, pair)

    def greet(seq, rep):
        pl.semaphore_signal(
            barrier, inc=1, device_id={"seq": seq, "rep": rep}, device_id_type=MESH
        )

    each(direct, 0, lambda step: greet(*place_of(step)))
    each(pair, 1, lambda step: greet(my_seq, partner_of(step)))

    small[0].wait()
    order_twice[...] = order[...] * 2
    load_spots.start()

    lane_head = lax.broadcasted_iota(jnp.int32, (1, width), 1) // head_dim
    near_heads = LANES // head_dim
    slabs = [slice(g * LANES, (g + 1) * LANES) for g in range(width // LANES)]
    near = lax.broadcasted_iota(jnp.int32, (1, LANES), 1) // head_dim
    head_lanes = [(near == h).astype(F32).astype(BF) for h in range(near_heads)]

    def by_head(block):
        return jnp.concatenate([block * lanes for lanes in head_lanes], axis=0)

    block_mean = jnp.where(
        lax.broadcasted_iota(jnp.int32, (width, width), 0) // head_dim
        == lax.broadcasted_iota(jnp.int32, (width, width), 1) // head_dim,
        1.0 / head_dim,
        0.0,
    ).astype(BF)

    def lane_scale(row):
        scale = jnp.zeros((1, width), F32)
        for h in range(heads):
            scale = jnp.where(lane_head == h, temps[row, h], scale)
        return scale * (LOG2E / math.sqrt(head_dim))

    def head_rms(values):
        return values * lax.rsqrt(dot((values * values).astype(BF), block_mean) + EPS)

    for i in range(chunks):
        enter(i).wait()
        block = points[pl.ds(i * chunk, chunk), :].astype(F32)
        for n in range(halves):
            wide[pl.ds(2 * i * chunk + n, chunk, stride=2), :] = block[:, slabs[n]]
    for load in small[1:]:
        load.wait()
    load_spots.wait()
    loads[0].wait()

    gain_a = gain_attn[...]
    q_scale = lane_scale(0)

    def gather_chunk(i):
        for r in range(i * chunk, (i + 1) * chunk):
            picked[pl.ds(2 * r, 2), :] = wide[pl.ds(spots[0, r], 2), :]

    def pool_chunk(i):
        sorted_rows = jnp.concatenate(
            [picked[pl.ds(2 * i * chunk + n, chunk, stride=2), :] for n in range(halves)], axis=1
        )
        spot = pl.ds(i * chunk, chunk)
        srt[spot, :] = sorted_rows.astype(BF)
        normed = rms(sorted_rows, gain_a).astype(BF)
        nrm[spot, :] = normed
        shape = (2 * tokens, chunk)
        token = lax.broadcasted_iota(jnp.int32, shape, 0)
        place = lax.broadcasted_iota(jnp.int32, shape, 1)
        half = jnp.zeros(shape, jnp.int32)
        for b in range(4):
            half = jnp.where(token // 2 == b, counts[i * 4 + b], half)
        half = jnp.clip(half - POOL * (token % 2), 0, POOL)
        offset = place - token * POOL
        take = jnp.where((offset >= 0) & (offset < half), 1.0, 0.0).astype(BF)
        total = dot(take, normed)[:tokens]
        half_f = half[:tokens, :width].astype(F32)
        stage[pl.ds(i * tokens, tokens), :] = jnp.where(
            half_f > 0.0, total / jnp.maximum(half_f, 1.0), NO_TOKEN
        )

    def qkv_chunk(i):
        spot = pl.ds(i * chunk, chunk)
        joined = dot(nrm[spot, :], w_qkv[...])
        queries[spot, :] = (head_rms(joined[:, :width]) * q_scale).astype(BF)
        keys[spot, :] = head_rms(joined[:, width : 2 * width]).astype(BF)
        values[spot, :] = joined[:, 2 * width :].astype(BF)

    gather_chunk(0)
    for i in range(1, chunks):
        gather_chunk(i)
        pool_chunk(i - 1)
    pool_chunk(chunks - 1)

    own_block = stage[...].astype(BF)
    tokens_all[me] = own_block

    pl.semaphore_wait(barrier, direct + pair - 1)

    def copy_of(block, send_sem, seq, rep):
        return pltpu.make_async_remote_copy(
            src_ref=tokens_all.at[block],
            dst_ref=tokens_all.at[block],
            send_sem=send_sem,
            recv_sem=recv_sem.at[block],
            device_id={"seq": seq, "rep": rep},
            device_id_type=MESH,
        )

    def spread(step):
        return copy_of(me, direct_send.at[step], *place_of(step))

    def forward(block, step):
        return copy_of(block, pair_send.at[block, step], my_seq, partner_of(step))

    def arrival(block):
        return copy_of(block, direct_send.at[0], *place_of(0))

    each(direct, 0, lambda step: spread(step).start())
    each(pair, 1, lambda step: forward(me, step).start())

    def block_of(step):
        seq, rep = place_of(direct - 1 - step)
        return seq * rep_n + rep

    def relay(step):
        block = block_of(step)
        arrival(block).wait_recv()
        each(pair, 1, lambda away: forward(block, away).start())

    for load in loads[1:]:
        load.wait()

    def ball_chunk(i):
        mixes = []
        for b in range(4):
            spot = pl.ds(i * chunk + b * BALL, BALL)
            q, k, v = queries[spot, :], keys[spot, :], values[spot, :]
            live = lax.broadcasted_iota(jnp.int32, (BALL, LANES), 0) < counts[i * 4 + b]
            there = jnp.where(live, 1.0, 0.0).astype(BF)
            alive = [there * lanes for lanes in head_lanes]
            ones = jnp.concatenate(alive, axis=0)
            slab_mixes = []
            for slab in slabs:
                weights = jnp.exp2(dot_t(q[:, slab], by_head(k[:, slab]))).astype(BF)
                seen = jnp.concatenate([v[:, slab] * lanes for lanes in alive], axis=0)
                mixed = dot(weights, jnp.concatenate([seen, ones], axis=1))
                slab_mixes.append((mixed[:, :LANES] / mixed[:, LANES:]).astype(BF))
            mixes.append(jnp.concatenate(slab_mixes, axis=1))
        fine = dot(jnp.concatenate(mixes, axis=0), w_out[...])
        spot = pl.ds(i * chunk, chunk)
        mid[spot, :] = (srt[spot, :].astype(F32) + fine).astype(BF)

    early = chunks // 2
    first = direct // 2
    qkv_chunk(0)
    for i in range(chunks):
        if i + 1 < chunks:
            qkv_chunk(i + 1)
        ball_chunk(i)
        if i == early - 1:
            each(first, 0, relay)
        if i == chunks - 2:
            each(direct, first, relay)

    own_tokens = jnp.where(own_block < NO_TOKEN / 2, own_block, 0.0).astype(BF)
    q_c = dot(own_tokens, c_qkv[:, :width])
    q_c = (head_rms(q_c) * lane_scale(1)).astype(BF)
    coarse_queries = [by_head(q_c[:, slab]) for slab in slabs]

    def gathered(step):
        rep = partner_of(step)
        each(pairs, 0, lambda away: each(seq_n, 0, lambda seq: arrival(
            seq * rep_n + lax.rem(rep + pair * away, rep_n)
        ).wait_recv()))

    each(pair, 1, gathered)

    group = math.gcd(peers, 16)

    def coarse_keys(g):
        block = tokens_all[pl.ds(g * group, group)].reshape(group * coarse_rows, width)
        there = block < NO_TOKEN / 2
        ones = jnp.where(there[:, :LANES], 1.0, 0.0).astype(BF)
        joined = dot(jnp.where(there, block, 0.0).astype(BF), c_qkv[:, width:])
        c_keys = head_rms(joined[:, :width]).astype(BF)
        c_values = joined[:, width:].astype(BF)
        sums = []
        for query, slab in zip(coarse_queries, slabs):
            weights = jnp.exp2(dot_t(query, c_keys[:, slab])).astype(BF)
            sums.append(dot(weights, jnp.concatenate([c_values[:, slab], ones], axis=1)))
        return sums

    if peers == group:
        sums = coarse_keys(0)
    else:
        sums = lax.fori_loop(
            0,
            peers // group,
            lambda g, total: [a + b for a, b in zip(total, coarse_keys(g))],
            [jnp.zeros((near_heads * coarse_rows, 2 * LANES), F32) for _ in slabs],
        )
    slab_mixes = []
    for total in sums:
        ratio = total[:, :LANES] / total[:, LANES:]
        mix = jnp.zeros((coarse_rows, LANES), F32)
        for h in range(near_heads):
            mix = jnp.where(near == h, ratio[h * coarse_rows : (h + 1) * coarse_rows], mix)
        slab_mixes.append(mix)
    mix = jnp.concatenate(slab_mixes, axis=1)
    coarse[...] = dot(mix.astype(BF), c_out[...])

    each(direct, 0, lambda step: spread(step).wait_send())
    each(pair, 1, lambda step: forward(me, step).wait_send())
    each(direct, 0, lambda step: each(
        pair, 1, lambda away: forward(block_of(step), away).wait_send()
    ))


def mlp_kernel(
    mid,
    coarse,
    order,
    gain_mlp,
    w_up,
    w_down,
    out,
    res,
    ready,
    packed,
    order_twice,
    spots,
    load_sem,
    out_sem,
):
    rows, width = mid.shape
    chunk = 4 * BALL
    chunks = rows // chunk
    tokens = chunk // POOL
    gain_half = gain_mlp[...] * 0.5

    order_twice[...] = order[...] * 2
    load_spots = pltpu.make_async_copy(order_twice, spots, load_sem)
    load_spots.start()

    def mlp_chunk(i):
        terms = coarse[pl.ds(i * tokens, tokens), :]
        spread = jnp.concatenate(
            [jnp.broadcast_to(terms[t : t + 1], (POOL, width)) for t in range(tokens)], axis=0
        )
        middle = mid[pl.ds(i * chunk, chunk), :].astype(F32) + spread
        mlp_in = rms(middle, gain_half).astype(BF)
        activated = gelu_of_half(dot(mlp_in, w_up[...]).astype(BF))
        result = middle + dot(activated, w_down[...])
        for n in range(width // LANES):
            res[pl.ds(2 * i * chunk + n, chunk, stride=2), :] = result[:, n * LANES : (n + 1) * LANES]

    def scatter_chunk(i):
        for r in range(i * chunk, (i + 1) * chunk):
            ready[pl.ds(spots[0, r], 2), :] = res[pl.ds(2 * r, 2), :]

    mlp_chunk(0)
    load_spots.wait()
    for i in range(1, chunks):
        scatter_chunk(i - 1)
        mlp_chunk(i)
    scatter_chunk(chunks - 1)

    def leave(i):
        spot = pl.ds(i * chunk, chunk)
        return pltpu.make_async_copy(packed.at[spot, :], out.at[spot, :], out_sem.at[i])

    for i in range(chunks):
        packed[pl.ds(i * chunk, chunk), :] = jnp.concatenate(
            [ready[pl.ds(2 * i * chunk + n, chunk, stride=2), :] for n in range(width // LANES)], axis=1
        ).astype(BF)
        leave(i).start()
    for i in range(chunks):
        leave(i).wait()


def on_device(
    sizes,
    points,
    ball_order,
    ball_counts,
    gain_attn,
    gain_mlp,
    head_temps,
    w_qkv,
    w_out,
    c_qkv,
    c_out,
    w_up,
    w_down,
):
    rows, width = points.shape
    heads = head_temps.shape[1]
    seq_n, rep_n = sizes
    peers = seq_n * rep_n
    coarse_rows = rows // POOL
    chunks = rows // (4 * BALL)
    vmem = pl.BlockSpec(memory_space=pltpu.VMEM)
    hbm = pl.BlockSpec(memory_space=pltpu.HBM)
    far = pl.BlockSpec(memory_space=pl.ANY)
    dma = pltpu.SemaphoreType.DMA
    tall = rows * width // LANES
    mid, coarse, gain_mid = pl.pallas_call(
        functools.partial(attend_kernel, (*sizes, heads)),
        out_shape=(
            jax.ShapeDtypeStruct((rows, width), BF),
            jax.ShapeDtypeStruct((coarse_rows, width), F32),
            jax.ShapeDtypeStruct((1, width), F32),
        ),
        in_specs=[hbm] * 10,
        out_specs=(vmem,) * 3,
        scratch_shapes=[
            pltpu.VMEM((rows, width), BF),
            pltpu.VMEM((1, rows), jnp.int32),
            pltpu.VMEM((1, rows), jnp.int32),
            pltpu.VMEM((1, width), F32),
            pltpu.SMEM((1, rows), jnp.int32),
            pltpu.SMEM(ball_counts.shape, jnp.int32),
            pltpu.SMEM(head_temps.shape, F32),
            pltpu.VMEM((tall, LANES), F32),
            pltpu.VMEM((tall, LANES), F32),
            pltpu.VMEM((rows, width), BF),
            pltpu.VMEM((rows, width), BF),
            pltpu.VMEM((rows, width), BF),
            pltpu.VMEM((rows, width), BF),
            pltpu.VMEM((rows, width), BF),
            pltpu.VMEM((coarse_rows, width), F32),
            pltpu.VMEM((peers, coarse_rows, width), BF),
            pltpu.VMEM(w_qkv.shape, BF),
            pltpu.VMEM(w_out.shape, BF),
            pltpu.VMEM(c_qkv.shape, BF),
            pltpu.VMEM(c_out.shape, BF),
            dma((chunks,)),
            dma((10,)),
            dma((peers,)),
            dma((peers, 2)),
            dma((peers,)),
        ],
        compiler_params=pltpu.CompilerParams(
            collective_id=0, has_side_effects=True, vmem_limit_bytes=VMEM_ATTEND
        ),
        name="attend",
    )(
        *(
            pltpu.with_memory_space_constraint(operand, pltpu.HBM)
            for operand in (
                points,
                ball_order,
                ball_counts,
                gain_attn.reshape(1, width),
                head_temps,
                w_qkv,
                w_out,
                c_qkv,
                c_out,
                gain_mlp.reshape(1, width),
            )
        )
    )
    return pl.pallas_call(
        mlp_kernel,
        out_shape=jax.ShapeDtypeStruct(points.shape, points.dtype),
        in_specs=[vmem] * 6,
        out_specs=far,
        scratch_shapes=[
            pltpu.VMEM((tall, LANES), F32),
            pltpu.VMEM((tall, LANES), F32),
            pltpu.VMEM((rows, width), BF),
            pltpu.VMEM((1, rows), jnp.int32),
            pltpu.SMEM((1, rows), jnp.int32),
            dma,
            dma((chunks,)),
        ],
        compiler_params=pltpu.CompilerParams(vmem_limit_bytes=VMEM_MLP),
        name="mlp",
    )(mid, coarse, ball_order, gain_mid, w_up, w_down)


def solution(mesh):
    rows = P(("groups", "seq", "rep"))
    sizes = (mesh.shape["seq"], mesh.shape["rep"])
    return jax.shard_map(
        functools.partial(on_device, sizes),
        mesh=mesh,
        in_specs=(P(("groups", "seq", "rep"), None),) * 2 + (rows,) + (P(),) * 9,
        out_specs=P(("groups", "seq", "rep"), None),
        check_vma=False,
    )
```

```python
import functools
import math

import jax
import jax.numpy as jnp
from jax import lax
from jax.experimental import pallas as pl
from jax.experimental.pallas import tpu as pltpu
from jax.sharding import PartitionSpec as P

BALL = 128
POOL = 64
EPS = 1e-06
VMEM_ATTEND = 32 << 20
VMEM_MLP = 32 << 20
LANES = 128
GELU_A = math.sqrt(2.0 / math.pi)
GELU_B = 0.044715 * math.sqrt(2.0 / math.pi)
NO_TOKEN = 1024.0
LOG2E = 1.4426950408889634
MESH = pl.DeviceIdType.MESH
BF = jnp.bfloat16
F32 = jnp.float32


def dot(a, b):
    return jnp.dot(a, b, preferred_element_type=F32)


def dot_t(a, b):
    return lax.dot_general(a, b, (((1,), (1,)), ((), ())), preferred_element_type=F32)


def gelu_of_half(half):
    inner = half * (2.0 * GELU_A + 8.0 * GELU_B * (half * half))
    return half + half * jnp.tanh(inner)


def rms(values, gain):
    return values * lax.rsqrt(jnp.mean(values * values, axis=-1, keepdims=True) + EPS) * gain


def attend_kernel(
    sizes,
    points_hbm,
    order_hbm,
    counts_hbm,
    gain_hbm,
    temps_hbm,
    w_qkv_hbm,
    w_out_hbm,
    c_qkv_hbm,
    c_out_hbm,
    gain_mlp_hbm,
    mid,
    coarse,
    gain_mid,
    points,
    order,
    order_twice,
    gain_attn,
    spots,
    counts,
    temps,
    wide,
    picked,
    srt,
    nrm,
    queries,
    keys,
    values,
    stage,
    tokens_all,
    w_qkv,
    w_out,
    c_qkv,
    c_out,
    points_sem,
    load_sem,
    direct_send,
    pair_send,
    recv_sem,
):
    seq_n, rep_n, heads = sizes
    peers = seq_n * rep_n
    rows, width = points.shape
    head_dim = width // heads
    chunk = 4 * BALL
    chunks = rows // chunk
    tokens = chunk // POOL
    coarse_rows = rows // POOL
    halves = width // LANES
    my_seq = lax.axis_index("seq")
    my_rep = lax.axis_index("rep")
    me = my_seq * rep_n + my_rep
    pair = 2 if rep_n % 2 == 0 else 1
    pairs = rep_n // pair
    direct = seq_n * pairs - 1

    small = [
        pltpu.make_async_copy(source, target, load_sem.at[n])
        for n, (source, target) in enumerate(
            [(order_hbm, order), (counts_hbm, counts), (temps_hbm, temps), (gain_hbm, gain_attn)]
        )
    ]
    loads = [
        pltpu.make_async_copy(source, target, load_sem.at[4 + n])
        for n, (source, target) in enumerate(
            [
                (w_qkv_hbm, w_qkv),
                (w_out_hbm, w_out),
                (c_qkv_hbm, c_qkv),
                (c_out_hbm, c_out),
                (gain_mlp_hbm, gain_mid),
            ]
        )
    ]
    load_spots = pltpu.make_async_copy(order_twice, spots, load_sem.at[9])

    def enter(i):
        spot = pl.ds(i * chunk, chunk)
        return pltpu.make_async_copy(points_hbm.at[spot, :], points.at[spot, :], points_sem.at[i])

    small[0].start()
    for i in range(chunks):
        enter(i).start()
    for load in small[1:] + loads:
        load.start()

    barrier = pltpu.get_barrier_semaphore()

    def each(count, first, act):
        def body(step, carry):
            act(step)
            return carry

        lax.fori_loop(first, count, body, 0)

    def seq_place(step):
        above = seq_n - 1 - my_seq
        rising = jnp.where(step < above, seq_n - 1 - step, step - above)
        falling = jnp.where(step < my_seq, step, seq_n - 1 - step + my_seq)
        return jnp.where(my_seq < seq_n // 2, rising, falling)

    def place_of(step):
        away = step // pairs
        seq = jnp.where(away < seq_n - 1, seq_place(away), my_seq)
        rep = lax.rem(my_rep + pair * (1 + lax.rem(step, pairs)), rep_n)
        return seq, rep

    def partner_of(step):
        return my_rep - lax.rem(my_rep, pair) + lax.rem(my_rep + step, pair)

    def greet(seq, rep):
        pl.semaphore_signal(
            barrier, inc=1, device_id={"seq": seq, "rep": rep}, device_id_type=MESH
        )

    each(direct, 0, lambda step: greet(*place_of(step)))
    each(pair, 1, lambda step: greet(my_seq, partner_of(step)))

    small[0].wait()
    order_twice[...] = order[...] * 2
    load_spots.start()

    lane_head = lax.broadcasted_iota(jnp.int32, (1, width), 1) // head_dim
    near_heads = LANES // head_dim
    slabs = [slice(g * LANES, (g + 1) * LANES) for g in range(width // LANES)]
    near = lax.broadcasted_iota(jnp.int32, (1, LANES), 1) // head_dim
    head_lanes = [(near == h).astype(F32).astype(BF) for h in range(near_heads)]

    def by_head(block):
        return jnp.concatenate([block * lanes for lanes in head_lanes], axis=0)

    block_mean = jnp.where(
        lax.broadcasted_iota(jnp.int32, (width, width), 0) // head_dim
        == lax.broadcasted_iota(jnp.int32, (width, width), 1) // head_dim,
        1.0 / head_dim,
        0.0,
    ).astype(BF)

    def lane_scale(row):
        scale = jnp.zeros((1, width), F32)
        for h in range(heads):
            scale = jnp.where(lane_head == h, temps[row, h], scale)
        return scale * (LOG2E / math.sqrt(head_dim))

    def head_rms(values):
        return values * lax.rsqrt(dot((values * values).astype(BF), block_mean) + EPS)

    for i in range(chunks):
        enter(i).wait()
        block = points[pl.ds(i * chunk, chunk), :].astype(F32)
        for n in range(halves):
            wide[pl.ds(2 * i * chunk + n, chunk, stride=2), :] = block[:, slabs[n]]
    for load in small[1:]:
        load.wait()
    load_spots.wait()
    loads[0].wait()

    gain_a = gain_attn[...]
    q_scale = lane_scale(0)

    def gather_chunk(i):
        for r in range(i * chunk, (i + 1) * chunk):
            picked[pl.ds(2 * r, 2), :] = wide[pl.ds(spots[0, r], 2), :]

    def pool_chunk(i):
        sorted_rows = jnp.concatenate(
            [picked[pl.ds(2 * i * chunk + n, chunk, stride=2), :] for n in range(halves)], axis=1
        )
        spot = pl.ds(i * chunk, chunk)
        srt[spot, :] = sorted_rows.astype(BF)
        normed = rms(sorted_rows, gain_a).astype(BF)
        nrm[spot, :] = normed
        shape = (2 * tokens, chunk)
        token = lax.broadcasted_iota(jnp.int32, shape, 0)
        place = lax.broadcasted_iota(jnp.int32, shape, 1)
        half = jnp.zeros(shape, jnp.int32)
        for b in range(4):
            half = jnp.where(token // 2 == b, counts[i * 4 + b], half)
        half = jnp.clip(half - POOL * (token % 2), 0, POOL)
        offset = place - token * POOL
        take = jnp.where((offset >= 0) & (offset < half), 1.0, 0.0).astype(BF)
        total = dot(take, normed)[:tokens]
        half_f = half[:tokens, :width].astype(F32)
        stage[pl.ds(i * tokens, tokens), :] = jnp.where(
            half_f > 0.0, total / jnp.maximum(half_f, 1.0), NO_TOKEN
        )

    def qkv_chunk(i):
        spot = pl.ds(i * chunk, chunk)
        joined = dot(nrm[spot, :], w_qkv[...])
        queries[spot, :] = (head_rms(joined[:, :width]) * q_scale).astype(BF)
        keys[spot, :] = head_rms(joined[:, width : 2 * width]).astype(BF)
        values[spot, :] = joined[:, 2 * width :].astype(BF)

    gather_chunk(0)
    for i in range(1, chunks):
        gather_chunk(i)
        pool_chunk(i - 1)
    pool_chunk(chunks - 1)

    own_block = stage[...].astype(BF)
    tokens_all[me] = own_block

    pl.semaphore_wait(barrier, direct + pair - 1)

    def copy_of(block, send_sem, seq, rep):
        return pltpu.make_async_remote_copy(
            src_ref=tokens_all.at[block],
            dst_ref=tokens_all.at[block],
            send_sem=send_sem,
            recv_sem=recv_sem.at[block],
            device_id={"seq": seq, "rep": rep},
            device_id_type=MESH,
        )

    def spread(step):
        return copy_of(me, direct_send.at[step], *place_of(step))

    def forward(block, step):
        return copy_of(block, pair_send.at[block, step], my_seq, partner_of(step))

    def arrival(block):
        return copy_of(block, direct_send.at[0], *place_of(0))

    each(direct, 0, lambda step: spread(step).start())
    each(pair, 1, lambda step: forward(me, step).start())

    def block_of(step):
        seq, rep = place_of(direct - 1 - step)
        return seq * rep_n + rep

    def relay(step):
        block = block_of(step)
        arrival(block).wait_recv()
        each(pair, 1, lambda away: forward(block, away).start())

    for load in loads[1:]:
        load.wait()

    def ball_chunk(i):
        mixes = []
        for b in range(4):
            spot = pl.ds(i * chunk + b * BALL, BALL)
            q, k, v = queries[spot, :], keys[spot, :], values[spot, :]
            live = lax.broadcasted_iota(jnp.int32, (BALL, LANES), 0) < counts[i * 4 + b]
            there = jnp.where(live, 1.0, 0.0).astype(BF)
            alive = [there * lanes for lanes in head_lanes]
            ones = jnp.concatenate(alive, axis=0)
            slab_mixes = []
            for slab in slabs:
                weights = jnp.exp2(dot_t(q[:, slab], by_head(k[:, slab]))).astype(BF)
                seen = jnp.concatenate([v[:, slab] * lanes for lanes in alive], axis=0)
                mixed = dot(weights, jnp.concatenate([seen, ones], axis=1))
                slab_mixes.append((mixed[:, :LANES] / mixed[:, LANES:]).astype(BF))
            mixes.append(jnp.concatenate(slab_mixes, axis=1))
        fine = dot(jnp.concatenate(mixes, axis=0), w_out[...])
        spot = pl.ds(i * chunk, chunk)
        mid[spot, :] = (srt[spot, :].astype(F32) + fine).astype(BF)

    first = direct // 2
    qkv_chunk(0)
    for i in range(chunks):
        if i + 1 < chunks:
            qkv_chunk(i + 1)
        ball_chunk(i)
        if i == chunks - 2:
            each(first, 0, relay)
    each(direct, first, relay)

    own_tokens = jnp.where(own_block < NO_TOKEN / 2, own_block, 0.0).astype(BF)
    q_c = dot(own_tokens, c_qkv[:, :width])
    q_c = (head_rms(q_c) * lane_scale(1)).astype(BF)
    coarse_queries = [by_head(q_c[:, slab]) for slab in slabs]

    def gathered(step):
        rep = partner_of(step)
        each(pairs, 0, lambda away: each(seq_n, 0, lambda seq: arrival(
            seq * rep_n + lax.rem(rep + pair * away, rep_n)
        ).wait_recv()))

    blocks = seq_n * pairs
    group = math.gcd(blocks, 8)

    def coarse_keys(side, g):
        members = [
            (g * group + t) // pairs * rep_n + (g * group + t) % pairs * pair + side
            for t in range(group)
        ]
        block = jnp.concatenate([tokens_all[member] for member in members], axis=0)
        there = block < NO_TOKEN / 2
        ones = jnp.where(there[:, :LANES], 1.0, 0.0).astype(BF)
        joined = dot(jnp.where(there, block, 0.0).astype(BF), c_qkv[:, width:])
        c_keys = head_rms(joined[:, :width]).astype(BF)
        c_values = joined[:, width:].astype(BF)
        sums = []
        for query, slab in zip(coarse_queries, slabs):
            weights = jnp.exp2(dot_t(query, c_keys[:, slab])).astype(BF)
            sums.append(dot(weights, jnp.concatenate([c_values[:, slab], ones], axis=1)))
        return sums

    def coarse_side(side):
        if blocks == group:
            return coarse_keys(side, 0)
        return lax.fori_loop(
            0,
            blocks // group,
            lambda g, total: [a + b for a, b in zip(total, coarse_keys(side, g))],
            [jnp.zeros((near_heads * coarse_rows, 2 * LANES), F32) for _ in slabs],
        )

    sums = coarse_side(lax.rem(my_rep, pair))
    each(pair, 1, gathered)
    if pair > 1:
        sums = [a + b for a, b in zip(sums, coarse_side(lax.rem(my_rep + 1, pair)))]
    slab_mixes = []
    for total in sums:
        ratio = total[:, :LANES] / total[:, LANES:]
        mix = jnp.zeros((coarse_rows, LANES), F32)
        for h in range(near_heads):
            mix = jnp.where(near == h, ratio[h * coarse_rows : (h + 1) * coarse_rows], mix)
        slab_mixes.append(mix)
    mix = jnp.concatenate(slab_mixes, axis=1)
    coarse[...] = dot(mix.astype(BF), c_out[...])

    each(direct, 0, lambda step: spread(step).wait_send())
    each(pair, 1, lambda step: forward(me, step).wait_send())
    each(direct, 0, lambda step: each(
        pair, 1, lambda away: forward(block_of(step), away).wait_send()
    ))


def mlp_kernel(
    mid,
    coarse,
    order,
    gain_mlp,
    w_up,
    w_down,
    out,
    res,
    ready,
    packed,
    order_twice,
    spots,
    load_sem,
    out_sem,
):
    rows, width = mid.shape
    chunk = 4 * BALL
    chunks = rows // chunk
    tokens = chunk // POOL
    gain_half = gain_mlp[...] * 0.5

    order_twice[...] = order[...] * 2
    load_spots = pltpu.make_async_copy(order_twice, spots, load_sem)
    load_spots.start()

    def mlp_chunk(i):
        terms = coarse[pl.ds(i * tokens, tokens), :]
        spread = jnp.concatenate(
            [jnp.broadcast_to(terms[t : t + 1], (POOL, width)) for t in range(tokens)], axis=0
        )
        middle = mid[pl.ds(i * chunk, chunk), :].astype(F32) + spread
        mlp_in = rms(middle, gain_half).astype(BF)
        activated = gelu_of_half(dot(mlp_in, w_up[...]).astype(BF))
        result = middle + dot(activated, w_down[...])
        for n in range(width // LANES):
            res[pl.ds(2 * i * chunk + n, chunk, stride=2), :] = result[:, n * LANES : (n + 1) * LANES]

    def scatter_chunk(i):
        for r in range(i * chunk, (i + 1) * chunk):
            ready[pl.ds(spots[0, r], 2), :] = res[pl.ds(2 * r, 2), :]

    mlp_chunk(0)
    load_spots.wait()
    for i in range(1, chunks):
        scatter_chunk(i - 1)
        mlp_chunk(i)
    scatter_chunk(chunks - 1)

    def leave(i):
        spot = pl.ds(i * chunk, chunk)
        return pltpu.make_async_copy(packed.at[spot, :], out.at[spot, :], out_sem.at[i])

    for i in range(chunks):
        packed[pl.ds(i * chunk, chunk), :] = jnp.concatenate(
            [ready[pl.ds(2 * i * chunk + n, chunk, stride=2), :] for n in range(width // LANES)], axis=1
        ).astype(BF)
        leave(i).start()
    for i in range(chunks):
        leave(i).wait()


def on_device(
    sizes,
    points,
    ball_order,
    ball_counts,
    gain_attn,
    gain_mlp,
    head_temps,
    w_qkv,
    w_out,
    c_qkv,
    c_out,
    w_up,
    w_down,
):
    rows, width = points.shape
    heads = head_temps.shape[1]
    seq_n, rep_n = sizes
    peers = seq_n * rep_n
    coarse_rows = rows // POOL
    chunks = rows // (4 * BALL)
    vmem = pl.BlockSpec(memory_space=pltpu.VMEM)
    hbm = pl.BlockSpec(memory_space=pltpu.HBM)
    far = pl.BlockSpec(memory_space=pl.ANY)
    dma = pltpu.SemaphoreType.DMA
    tall = rows * width // LANES
    mid, coarse, gain_mid = pl.pallas_call(
        functools.partial(attend_kernel, (*sizes, heads)),
        out_shape=(
            jax.ShapeDtypeStruct((rows, width), BF),
            jax.ShapeDtypeStruct((coarse_rows, width), F32),
            jax.ShapeDtypeStruct((1, width), F32),
        ),
        in_specs=[hbm] * 10,
        out_specs=(vmem,) * 3,
        scratch_shapes=[
            pltpu.VMEM((rows, width), BF),
            pltpu.VMEM((1, rows), jnp.int32),
            pltpu.VMEM((1, rows), jnp.int32),
            pltpu.VMEM((1, width), F32),
            pltpu.SMEM((1, rows), jnp.int32),
            pltpu.SMEM(ball_counts.shape, jnp.int32),
            pltpu.SMEM(head_temps.shape, F32),
            pltpu.VMEM((tall, LANES), F32),
            pltpu.VMEM((tall, LANES), F32),
            pltpu.VMEM((rows, width), BF),
            pltpu.VMEM((rows, width), BF),
            pltpu.VMEM((rows, width), BF),
            pltpu.VMEM((rows, width), BF),
            pltpu.VMEM((rows, width), BF),
            pltpu.VMEM((coarse_rows, width), F32),
            pltpu.VMEM((peers, coarse_rows, width), BF),
            pltpu.VMEM(w_qkv.shape, BF),
            pltpu.VMEM(w_out.shape, BF),
            pltpu.VMEM(c_qkv.shape, BF),
            pltpu.VMEM(c_out.shape, BF),
            dma((chunks,)),
            dma((10,)),
            dma((peers,)),
            dma((peers, 2)),
            dma((peers,)),
        ],
        compiler_params=pltpu.CompilerParams(
            collective_id=0, has_side_effects=True, vmem_limit_bytes=VMEM_ATTEND
        ),
        name="attend",
    )(
        *(
            pltpu.with_memory_space_constraint(operand, pltpu.HBM)
            for operand in (
                points,
                ball_order,
                ball_counts,
                gain_attn.reshape(1, width),
                head_temps,
                w_qkv,
                w_out,
                c_qkv,
                c_out,
                gain_mlp.reshape(1, width),
            )
        )
    )
    return pl.pallas_call(
        mlp_kernel,
        out_shape=jax.ShapeDtypeStruct(points.shape, points.dtype),
        in_specs=[vmem] * 6,
        out_specs=far,
        scratch_shapes=[
            pltpu.VMEM((tall, LANES), F32),
            pltpu.VMEM((tall, LANES), F32),
            pltpu.VMEM((rows, width), BF),
            pltpu.VMEM((1, rows), jnp.int32),
            pltpu.SMEM((1, rows), jnp.int32),
            dma,
            dma((chunks,)),
        ],
        compiler_params=pltpu.CompilerParams(vmem_limit_bytes=VMEM_MLP),
        name="mlp",
    )(mid, coarse, ball_order, gain_mid, w_up, w_down)


def solution(mesh):
    rows = P(("groups", "seq", "rep"))
    sizes = (mesh.shape["seq"], mesh.shape["rep"])
    return jax.shard_map(
        functools.partial(on_device, sizes),
        mesh=mesh,
        in_specs=(P(("groups", "seq", "rep"), None),) * 2 + (rows,) + (P(),) * 9,
        out_specs=P(("groups", "seq", "rep"), None),
        check_vma=False,
    )
```

```python
import functools
import math

import jax
import jax.numpy as jnp
from jax import lax
from jax.experimental import pallas as pl
from jax.experimental.pallas import tpu as pltpu
from jax.sharding import PartitionSpec as P

BALL = 128
POOL = 64
EPS = 1e-06
VMEM_ATTEND = 32 << 20
VMEM_MLP = 32 << 20
LANES = 128
GELU_A = math.sqrt(2.0 / math.pi)
GELU_B = 0.044715 * math.sqrt(2.0 / math.pi)
NO_TOKEN = 1024.0
GELU_SCALE = (8.0 * GELU_B) ** (1.0 / 3.0)
LOG2E = 1.4426950408889634
MESH = pl.DeviceIdType.MESH
BF = jnp.bfloat16
F32 = jnp.float32


def dot(a, b):
    return jnp.dot(a, b, preferred_element_type=F32)


def dot_t(a, b):
    return lax.dot_general(a, b, (((1,), (1,)), ((), ())), preferred_element_type=F32)


def scaled_gelu(scaled):
    return scaled + scaled * jnp.tanh(scaled * (2.0 * GELU_A / GELU_SCALE + scaled * scaled))


def rms(values, gain):
    return values * lax.rsqrt(jnp.mean(values * values, axis=-1, keepdims=True) + EPS) * gain


def attend_kernel(
    sizes,
    points_hbm,
    order_hbm,
    counts_hbm,
    gain_hbm,
    temps_hbm,
    w_qkv_hbm,
    w_out_hbm,
    c_qkv_hbm,
    c_out_hbm,
    gain_mlp_hbm,
    w_up_hbm,
    w_down_hbm,
    mid,
    coarse,
    gain_mid,
    upward,
    w_up,
    w_down,
    order,
    points,
    order_twice,
    gain_attn,
    spots,
    counts,
    temps,
    wide,
    picked,
    srt,
    nrm,
    queries,
    keys,
    values,
    stage,
    tokens_all,
    w_qkv,
    w_out,
    c_qkv,
    c_out,
    points_sem,
    load_sem,
    direct_send,
    pair_send,
    recv_sem,
):
    seq_n, rep_n, heads = sizes
    peers = seq_n * rep_n
    rows, width = points.shape
    head_dim = width // heads
    chunk = 4 * BALL
    chunks = rows // chunk
    tokens = chunk // POOL
    coarse_rows = rows // POOL
    halves = width // LANES
    my_seq = lax.axis_index("seq")
    my_rep = lax.axis_index("rep")
    me = my_seq * rep_n + my_rep
    pair = 2 if rep_n % 2 == 0 else 1
    pairs = rep_n // pair
    direct = seq_n * pairs - 1

    small = [
        pltpu.make_async_copy(source, target, load_sem.at[n])
        for n, (source, target) in enumerate(
            [(order_hbm, order), (counts_hbm, counts), (temps_hbm, temps), (gain_hbm, gain_attn)]
        )
    ]
    loads = [
        pltpu.make_async_copy(source, target, load_sem.at[4 + n])
        for n, (source, target) in enumerate(
            [
                (w_qkv_hbm, w_qkv),
                (w_out_hbm, w_out),
                (c_qkv_hbm, c_qkv),
                (c_out_hbm, c_out),
                (gain_mlp_hbm, gain_mid),
                (w_up_hbm, w_up),
                (w_down_hbm, w_down),
            ]
        )
    ]
    load_spots = pltpu.make_async_copy(order_twice, spots, load_sem.at[11])

    def enter(i):
        spot = pl.ds(i * chunk, chunk)
        return pltpu.make_async_copy(points_hbm.at[spot, :], points.at[spot, :], points_sem.at[i])

    small[0].start()
    for i in range(chunks):
        enter(i).start()
    for load in small[1:] + loads:
        load.start()

    barrier = pltpu.get_barrier_semaphore()

    def each(count, first, act):
        def body(step, carry):
            act(step)
            return carry

        lax.fori_loop(first, count, body, 0)

    def seq_place(step):
        above = seq_n - 1 - my_seq
        rising = jnp.where(step < above, seq_n - 1 - step, step - above)
        falling = jnp.where(step < my_seq, step, seq_n - 1 - step + my_seq)
        return jnp.where(my_seq < seq_n // 2, rising, falling)

    def place_of(step):
        away = step // pairs
        seq = jnp.where(away < seq_n - 1, seq_place(away), my_seq)
        rep = lax.rem(my_rep + pair * (1 + lax.rem(step, pairs)), rep_n)
        return seq, rep

    def partner_of(step):
        return my_rep - lax.rem(my_rep, pair) + lax.rem(my_rep + step, pair)

    def greet(seq, rep):
        pl.semaphore_signal(
            barrier, inc=1, device_id={"seq": seq, "rep": rep}, device_id_type=MESH
        )

    each(direct, 0, lambda step: greet(*place_of(step)))
    each(pair, 1, lambda step: greet(my_seq, partner_of(step)))

    small[0].wait()
    order_twice[...] = order[...] * 2
    load_spots.start()

    lane_head = lax.broadcasted_iota(jnp.int32, (1, width), 1) // head_dim
    near_heads = LANES // head_dim
    slabs = [slice(g * LANES, (g + 1) * LANES) for g in range(width // LANES)]
    near = lax.broadcasted_iota(jnp.int32, (1, LANES), 1) // head_dim
    head_lanes = [(near == h).astype(F32).astype(BF) for h in range(near_heads)]

    def by_head(block):
        return jnp.concatenate([block * lanes for lanes in head_lanes], axis=0)

    block_mean = jnp.where(
        lax.broadcasted_iota(jnp.int32, (width, width), 0) // head_dim
        == lax.broadcasted_iota(jnp.int32, (width, width), 1) // head_dim,
        1.0 / head_dim,
        0.0,
    ).astype(BF)

    def lane_scale(row):
        scale = jnp.zeros((1, width), F32)
        for h in range(heads):
            scale = jnp.where(lane_head == h, temps[row, h], scale)
        return scale * (LOG2E / math.sqrt(head_dim))

    def head_rms(values):
        return values * lax.rsqrt(dot((values * values).astype(BF), block_mean) + EPS)

    for i in range(chunks):
        enter(i).wait()
        block = points[pl.ds(i * chunk, chunk), :].astype(F32)
        for n in range(halves):
            wide[pl.ds(2 * i * chunk + n, chunk, stride=2), :] = block[:, slabs[n]]
    for load in small[1:]:
        load.wait()
    load_spots.wait()
    loads[0].wait()

    gain_a = gain_attn[...]
    q_scale = lane_scale(0)

    def gather_chunk(i):
        for r in range(i * chunk, (i + 1) * chunk):
            picked[pl.ds(2 * r, 2), :] = wide[pl.ds(spots[0, r], 2), :]

    def pool_chunk(i):
        sorted_rows = jnp.concatenate(
            [picked[pl.ds(2 * i * chunk + n, chunk, stride=2), :] for n in range(halves)], axis=1
        )
        spot = pl.ds(i * chunk, chunk)
        srt[spot, :] = sorted_rows.astype(BF)
        normed = rms(sorted_rows, gain_a).astype(BF)
        nrm[spot, :] = normed
        shape = (2 * tokens, chunk)
        token = lax.broadcasted_iota(jnp.int32, shape, 0)
        place = lax.broadcasted_iota(jnp.int32, shape, 1)
        half = jnp.zeros(shape, jnp.int32)
        for b in range(4):
            half = jnp.where(token // 2 == b, counts[i * 4 + b], half)
        half = jnp.clip(half - POOL * (token % 2), 0, POOL)
        offset = place - token * POOL
        take = jnp.where((offset >= 0) & (offset < half), 1.0, 0.0).astype(BF)
        total = dot(take, normed)[:tokens]
        half_f = half[:tokens, :width].astype(F32)
        stage[pl.ds(i * tokens, tokens), :] = jnp.where(
            half_f > 0.0, total / jnp.maximum(half_f, 1.0), NO_TOKEN
        )

    def qkv_chunk(i):
        spot = pl.ds(i * chunk, chunk)
        joined = dot(nrm[spot, :], w_qkv[...])
        queries[spot, :] = (head_rms(joined[:, :width]) * q_scale).astype(BF)
        keys[spot, :] = head_rms(joined[:, width : 2 * width]).astype(BF)
        values[spot, :] = joined[:, 2 * width :].astype(BF)

    gather_chunk(0)
    for i in range(1, chunks):
        gather_chunk(i)
        pool_chunk(i - 1)
    pool_chunk(chunks - 1)

    own_block = stage[...].astype(BF)
    tokens_all[me] = own_block

    pl.semaphore_wait(barrier, direct + pair - 1)

    def copy_of(block, send_sem, seq, rep):
        return pltpu.make_async_remote_copy(
            src_ref=tokens_all.at[block],
            dst_ref=tokens_all.at[block],
            send_sem=send_sem,
            recv_sem=recv_sem.at[block],
            device_id={"seq": seq, "rep": rep},
            device_id_type=MESH,
        )

    def spread(step):
        return copy_of(me, direct_send.at[step], *place_of(step))

    def forward(block, step):
        return copy_of(block, pair_send.at[block, step], my_seq, partner_of(step))

    def arrival(block):
        return copy_of(block, direct_send.at[0], *place_of(0))

    each(direct, 0, lambda step: spread(step).start())
    each(pair, 1, lambda step: forward(me, step).start())

    def block_of(step):
        seq, rep = place_of(direct - 1 - step)
        return seq * rep_n + rep

    def relay(step):
        block = block_of(step)
        arrival(block).wait_recv()
        each(pair, 1, lambda away: forward(block, away).start())

    for load in loads[1:]:
        load.wait()

    def ball_chunk(i):
        mixes = []
        for b in range(4):
            spot = pl.ds(i * chunk + b * BALL, BALL)
            q, k, v = queries[spot, :], keys[spot, :], values[spot, :]
            live = lax.broadcasted_iota(jnp.int32, (BALL, LANES), 0) < counts[i * 4 + b]
            there = jnp.where(live, 1.0, 0.0).astype(BF)
            alive = [there * lanes for lanes in head_lanes]
            ones = jnp.concatenate(alive, axis=0)
            slab_mixes = []
            for slab in slabs:
                weights = jnp.exp2(dot_t(q[:, slab], by_head(k[:, slab]))).astype(BF)
                seen = jnp.concatenate([v[:, slab] * lanes for lanes in alive], axis=0)
                mixed = dot(weights, jnp.concatenate([seen, ones], axis=1))
                slab_mixes.append((mixed[:, :LANES] / mixed[:, LANES:]).astype(BF))
            mixes.append(jnp.concatenate(slab_mixes, axis=1))
        fine = dot(jnp.concatenate(mixes, axis=0), w_out[...])
        spot = pl.ds(i * chunk, chunk)
        near_mid = srt[spot, :].astype(F32) + fine
        mid[spot, :] = near_mid.astype(BF)
        upward[spot, :] = dot((near_mid * (gain_mid[...] * (0.5 * GELU_SCALE))).astype(BF), w_up[...]).astype(BF)

    first = direct // 2
    qkv_chunk(0)
    for i in range(chunks):
        if i + 1 < chunks:
            qkv_chunk(i + 1)
        ball_chunk(i)
        if i == chunks - 2:
            each(first, 0, relay)
    each(direct, first, relay)

    own_tokens = jnp.where(own_block < NO_TOKEN / 2, own_block, 0.0).astype(BF)
    q_c = dot(own_tokens, c_qkv[:, :width])
    q_c = (head_rms(q_c) * lane_scale(1)).astype(BF)
    coarse_queries = [by_head(q_c[:, slab]) for slab in slabs]

    def gathered(step):
        rep = partner_of(step)
        each(pairs, 0, lambda away: each(seq_n, 0, lambda seq: arrival(
            seq * rep_n + lax.rem(rep + pair * away, rep_n)
        ).wait_recv()))

    blocks = seq_n * pairs
    group = math.gcd(blocks, 8)

    def coarse_keys(side, g):
        members = [
            (g * group + t) // pairs * rep_n + (g * group + t) % pairs * pair + side
            for t in range(group)
        ]
        block = jnp.concatenate([tokens_all[member] for member in members], axis=0)
        there = block < NO_TOKEN / 2
        ones = jnp.where(there[:, :LANES], 1.0, 0.0).astype(BF)
        joined = dot(jnp.where(there, block, 0.0).astype(BF), c_qkv[:, width:])
        c_keys = head_rms(joined[:, :width]).astype(BF)
        c_values = joined[:, width:].astype(BF)
        sums = []
        for query, slab in zip(coarse_queries, slabs):
            weights = jnp.exp2(dot_t(query, c_keys[:, slab])).astype(BF)
            sums.append(dot(weights, jnp.concatenate([c_values[:, slab], ones], axis=1)))
        return sums

    def coarse_side(side):
        if blocks == group:
            return coarse_keys(side, 0)
        return lax.fori_loop(
            0,
            blocks // group,
            lambda g, total: [a + b for a, b in zip(total, coarse_keys(side, g))],
            [jnp.zeros((near_heads * coarse_rows, 2 * LANES), F32) for _ in slabs],
        )

    sums = coarse_side(lax.rem(my_rep, pair))
    each(pair, 1, gathered)
    if pair > 1:
        sums = [a + b for a, b in zip(sums, coarse_side(lax.rem(my_rep + 1, pair)))]
    slab_mixes = []
    for total in sums:
        ratio = total[:, :LANES] / total[:, LANES:]
        mix = jnp.zeros((coarse_rows, LANES), F32)
        for h in range(near_heads):
            mix = jnp.where(near == h, ratio[h * coarse_rows : (h + 1) * coarse_rows], mix)
        slab_mixes.append(mix)
    mix = jnp.concatenate(slab_mixes, axis=1)
    coarse[...] = dot(mix.astype(BF), c_out[...])

    each(direct, 0, lambda step: spread(step).wait_send())
    each(pair, 1, lambda step: forward(me, step).wait_send())
    each(direct, 0, lambda step: each(
        pair, 1, lambda away: forward(block_of(step), away).wait_send()
    ))


def mlp_kernel(
    mid,
    coarse,
    gain_mlp,
    upward,
    w_up,
    w_down,
    order,
    out,
    coarse_up,
    res,
    ready,
    packed,
    order_twice,
    spots,
    load_sem,
    out_sem,
):
    rows, width = mid.shape
    chunk = 4 * BALL
    chunks = rows // chunk
    tokens = chunk // POOL
    ffn = upward.shape[1]

    order_twice[...] = order[...] * 2
    load_spots = pltpu.make_async_copy(order_twice, spots, load_sem)
    load_spots.start()
    coarse_up[...] = dot((coarse[...] * (gain_mlp[...] * (0.5 * GELU_SCALE))).astype(BF), w_up[...])

    def mlp_chunk(i):
        terms = coarse[pl.ds(i * tokens, tokens), :]
        spread = jnp.concatenate(
            [jnp.broadcast_to(terms[t : t + 1], (POOL, width)) for t in range(tokens)], axis=0
        )
        middle = mid[pl.ds(i * chunk, chunk), :].astype(F32) + spread
        scale = lax.rsqrt(jnp.mean(middle * middle, axis=-1, keepdims=True) + EPS)
        scale = jnp.broadcast_to(scale, (chunk, LANES)).astype(BF)
        lifts = []
        for t in range(tokens):
            lift = coarse_up[pl.ds(i * tokens + t, 1), :]
            lifts += [jnp.broadcast_to(lift, (16, ffn)).astype(BF)] * (POOL // 16)
        half = upward[pl.ds(i * chunk, chunk), :] + jnp.concatenate(lifts, axis=0)
        half = half * jnp.concatenate([scale] * (ffn // LANES), axis=1)
        activated = scaled_gelu(half)
        down = jnp.concatenate(
            [dot(activated[: chunk // 2], w_down[...]), dot(activated[chunk // 2 :], w_down[...])],
            axis=0,
        )
        result = middle + down * (1.0 / GELU_SCALE)
        for n in range(width // LANES):
            res[pl.ds(2 * i * chunk + n, chunk, stride=2), :] = result[:, n * LANES : (n + 1) * LANES]

    def scatter_chunk(i):
        for r in range(i * chunk, (i + 1) * chunk):
            ready[pl.ds(spots[0, r], 2), :] = res[pl.ds(2 * r, 2), :]

    mlp_chunk(0)
    load_spots.wait()
    for i in range(1, chunks):
        scatter_chunk(i - 1)
        mlp_chunk(i)
    scatter_chunk(chunks - 1)

    def leave(i):
        spot = pl.ds(i * chunk, chunk)
        return pltpu.make_async_copy(packed.at[spot, :], out.at[spot, :], out_sem.at[i])

    for i in range(chunks):
        packed[pl.ds(i * chunk, chunk), :] = jnp.concatenate(
            [ready[pl.ds(2 * i * chunk + n, chunk, stride=2), :] for n in range(width // LANES)], axis=1
        ).astype(BF)
        leave(i).start()
    for i in range(chunks):
        leave(i).wait()


def on_device(
    sizes,
    points,
    ball_order,
    ball_counts,
    gain_attn,
    gain_mlp,
    head_temps,
    w_qkv,
    w_out,
    c_qkv,
    c_out,
    w_up,
    w_down,
):
    rows, width = points.shape
    heads = head_temps.shape[1]
    seq_n, rep_n = sizes
    peers = seq_n * rep_n
    coarse_rows = rows // POOL
    chunks = rows // (4 * BALL)
    vmem = pl.BlockSpec(memory_space=pltpu.VMEM)
    hbm = pl.BlockSpec(memory_space=pltpu.HBM)
    far = pl.BlockSpec(memory_space=pl.ANY)
    dma = pltpu.SemaphoreType.DMA
    tall = rows * width // LANES
    mid, coarse, *rest = pl.pallas_call(
        functools.partial(attend_kernel, (*sizes, heads)),
        out_shape=(
            jax.ShapeDtypeStruct((rows, width), BF),
            jax.ShapeDtypeStruct((coarse_rows, width), F32),
            jax.ShapeDtypeStruct((1, width), F32),
            jax.ShapeDtypeStruct((rows, w_up.shape[1]), BF),
            jax.ShapeDtypeStruct(w_up.shape, BF),
            jax.ShapeDtypeStruct(w_down.shape, BF),
            jax.ShapeDtypeStruct((1, rows), jnp.int32),
        ),
        in_specs=[hbm] * 12,
        out_specs=(vmem,) * 7,
        scratch_shapes=[
            pltpu.VMEM((rows, width), BF),
            pltpu.VMEM((1, rows), jnp.int32),
            pltpu.VMEM((1, width), F32),
            pltpu.SMEM((1, rows), jnp.int32),
            pltpu.SMEM(ball_counts.shape, jnp.int32),
            pltpu.SMEM(head_temps.shape, F32),
            pltpu.VMEM((tall, LANES), F32),
            pltpu.VMEM((tall, LANES), F32),
            pltpu.VMEM((rows, width), BF),
            pltpu.VMEM((rows, width), BF),
            pltpu.VMEM((rows, width), BF),
            pltpu.VMEM((rows, width), BF),
            pltpu.VMEM((rows, width), BF),
            pltpu.VMEM((coarse_rows, width), F32),
            pltpu.VMEM((peers, coarse_rows, width), BF),
            pltpu.VMEM(w_qkv.shape, BF),
            pltpu.VMEM(w_out.shape, BF),
            pltpu.VMEM(c_qkv.shape, BF),
            pltpu.VMEM(c_out.shape, BF),
            dma((chunks,)),
            dma((12,)),
            dma((peers,)),
            dma((peers, 2)),
            dma((peers,)),
        ],
        compiler_params=pltpu.CompilerParams(
            collective_id=0, has_side_effects=True, vmem_limit_bytes=VMEM_ATTEND
        ),
        name="attend",
    )(
        *(
            pltpu.with_memory_space_constraint(operand, pltpu.HBM)
            for operand in (
                points,
                ball_order,
                ball_counts,
                gain_attn.reshape(1, width),
                head_temps,
                w_qkv,
                w_out,
                c_qkv,
                c_out,
                gain_mlp.reshape(1, width),
                w_up,
                w_down,
            )
        )
    )
    return pl.pallas_call(
        mlp_kernel,
        out_shape=jax.ShapeDtypeStruct(points.shape, points.dtype),
        in_specs=[vmem] * 7,
        out_specs=far,
        scratch_shapes=[
            pltpu.VMEM((coarse_rows, w_up.shape[1]), F32),
            pltpu.VMEM((tall, LANES), F32),
            pltpu.VMEM((tall, LANES), F32),
            pltpu.VMEM((rows, width), BF),
            pltpu.VMEM((1, rows), jnp.int32),
            pltpu.SMEM((1, rows), jnp.int32),
            dma,
            dma((chunks,)),
        ],
        compiler_params=pltpu.CompilerParams(vmem_limit_bytes=VMEM_MLP),
        name="mlp",
    )(mid, coarse, *rest)


def solution(mesh):
    rows = P(("groups", "seq", "rep"))
    sizes = (mesh.shape["seq"], mesh.shape["rep"])
    return jax.shard_map(
        functools.partial(on_device, sizes),
        mesh=mesh,
        in_specs=(P(("groups", "seq", "rep"), None),) * 2 + (rows,) + (P(),) * 9,
        out_specs=P(("groups", "seq", "rep"), None),
        check_vma=False,
    )
```

```python
import functools
import math

import jax
import jax.numpy as jnp
from jax import lax
from jax.experimental import pallas as pl
from jax.experimental.pallas import tpu as pltpu
from jax.sharding import PartitionSpec as P

BALL = 128
POOL = 64
EPS = 1e-06
VMEM_ATTEND = 32 << 20
VMEM_MLP = 32 << 20
LANES = 128
GELU_A = math.sqrt(2.0 / math.pi)
GELU_B = 0.044715 * math.sqrt(2.0 / math.pi)
NO_TOKEN = 1024.0
LOG2E = 1.4426950408889634
MESH = pl.DeviceIdType.MESH
BF = jnp.bfloat16
F32 = jnp.float32


def dot(a, b):
    return jnp.dot(a, b, preferred_element_type=F32)


def dot_t(a, b):
    return lax.dot_general(a, b, (((1,), (1,)), ((), ())), preferred_element_type=F32)


def gelu_of_half(half):
    inner = half * (2.0 * GELU_A + 8.0 * GELU_B * (half * half))
    return half + half * jnp.tanh(inner)


def rms(values, gain):
    return values * lax.rsqrt(jnp.mean(values * values, axis=-1, keepdims=True) + EPS) * gain


def attend_kernel(
    sizes,
    points_hbm,
    order_hbm,
    counts_hbm,
    gain_hbm,
    temps_hbm,
    w_qkv_hbm,
    w_out_hbm,
    c_qkv_hbm,
    c_out_hbm,
    gain_mlp_hbm,
    mid,
    coarse,
    gain_mid,
    points,
    order,
    order_twice,
    gain_attn,
    spots,
    counts,
    temps,
    wide,
    picked,
    srt,
    nrm,
    queries,
    keys,
    values,
    stage,
    tokens_all,
    w_qkv,
    w_out,
    c_qkv,
    c_out,
    points_sem,
    load_sem,
    direct_send,
    pair_send,
    recv_sem,
):
    seq_n, rep_n, heads = sizes
    peers = seq_n * rep_n
    rows, width = points.shape
    head_dim = width // heads
    chunk = 4 * BALL
    chunks = rows // chunk
    tokens = chunk // POOL
    coarse_rows = rows // POOL
    halves = width // LANES
    my_seq = lax.axis_index("seq")
    my_rep = lax.axis_index("rep")
    me = my_seq * rep_n + my_rep
    pair = 2 if rep_n % 2 == 0 else 1
    pairs = rep_n // pair
    direct = seq_n * pairs - 1
    parts = 2 if chunks % 2 == 0 and chunks > 2 else 1
    part_chunks = chunks // parts
    part_rows = coarse_rows // parts

    small = [
        pltpu.make_async_copy(source, target, load_sem.at[n])
        for n, (source, target) in enumerate(
            [(order_hbm, order), (counts_hbm, counts), (temps_hbm, temps), (gain_hbm, gain_attn)]
        )
    ]
    loads = [
        pltpu.make_async_copy(source, target, load_sem.at[4 + n])
        for n, (source, target) in enumerate(
            [
                (w_qkv_hbm, w_qkv),
                (w_out_hbm, w_out),
                (c_qkv_hbm, c_qkv),
                (c_out_hbm, c_out),
                (gain_mlp_hbm, gain_mid),
            ]
        )
    ]
    load_spots = pltpu.make_async_copy(order_twice, spots, load_sem.at[9])

    def enter(i):
        spot = pl.ds(i * chunk, chunk)
        return pltpu.make_async_copy(points_hbm.at[spot, :], points.at[spot, :], points_sem.at[i])

    small[0].start()
    for i in range(chunks):
        enter(i).start()
    for load in small[1:] + loads:
        load.start()

    barrier = pltpu.get_barrier_semaphore()

    def each(count, first, act):
        def body(step, carry):
            act(step)
            return carry

        lax.fori_loop(first, count, body, 0)

    def seq_place(step):
        above = seq_n - 1 - my_seq
        rising = jnp.where(step < above, seq_n - 1 - step, step - above)
        falling = jnp.where(step < my_seq, step, seq_n - 1 - step + my_seq)
        return jnp.where(my_seq < seq_n // 2, rising, falling)

    def place_of(step):
        away = step // pairs
        seq = jnp.where(away < seq_n - 1, seq_place(away), my_seq)
        rep = lax.rem(my_rep + pair * (1 + lax.rem(step, pairs)), rep_n)
        return seq, rep

    def partner_of(step):
        return my_rep - lax.rem(my_rep, pair) + lax.rem(my_rep + step, pair)

    def greet(seq, rep):
        pl.semaphore_signal(
            barrier, inc=1, device_id={"seq": seq, "rep": rep}, device_id_type=MESH
        )

    each(direct, 0, lambda step: greet(*place_of(step)))
    each(pair, 1, lambda step: greet(my_seq, partner_of(step)))

    small[0].wait()
    order_twice[...] = order[...] * 2
    load_spots.start()

    lane_head = lax.broadcasted_iota(jnp.int32, (1, width), 1) // head_dim
    near_heads = LANES // head_dim
    slabs = [slice(g * LANES, (g + 1) * LANES) for g in range(width // LANES)]
    near = lax.broadcasted_iota(jnp.int32, (1, LANES), 1) // head_dim
    head_lanes = [(near == h).astype(F32).astype(BF) for h in range(near_heads)]

    def by_head(block):
        return jnp.concatenate([block * lanes for lanes in head_lanes], axis=0)

    block_mean = jnp.where(
        lax.broadcasted_iota(jnp.int32, (width, width), 0) // head_dim
        == lax.broadcasted_iota(jnp.int32, (width, width), 1) // head_dim,
        1.0 / head_dim,
        0.0,
    ).astype(BF)

    def lane_scale(row):
        scale = jnp.zeros((1, width), F32)
        for h in range(heads):
            scale = jnp.where(lane_head == h, temps[row, h], scale)
        return scale * (LOG2E / math.sqrt(head_dim))

    def head_rms(values):
        return values * lax.rsqrt(dot((values * values).astype(BF), block_mean) + EPS)

    for i in range(chunks):
        enter(i).wait()
        block = points[pl.ds(i * chunk, chunk), :].astype(F32)
        for n in range(halves):
            wide[pl.ds(2 * i * chunk + n, chunk, stride=2), :] = block[:, slabs[n]]
    for load in small[1:]:
        load.wait()
    load_spots.wait()
    loads[0].wait()

    gain_a = gain_attn[...]
    q_scale = lane_scale(0)

    def gather_rows(first_row, count):
        for r in range(first_row, first_row + count):
            picked[pl.ds(2 * r, 2), :] = wide[pl.ds(spots[0, r], 2), :]

    def pool_chunk(i):
        sorted_rows = jnp.concatenate(
            [picked[pl.ds(2 * i * chunk + n, chunk, stride=2), :] for n in range(halves)], axis=1
        )
        spot = pl.ds(i * chunk, chunk)
        srt[spot, :] = sorted_rows.astype(BF)
        normed = rms(sorted_rows, gain_a).astype(BF)
        nrm[spot, :] = normed
        shape = (2 * tokens, chunk)
        token = lax.broadcasted_iota(jnp.int32, shape, 0)
        place = lax.broadcasted_iota(jnp.int32, shape, 1)
        half = jnp.zeros(shape, jnp.int32)
        for b in range(4):
            half = jnp.where(token // 2 == b, counts[i * 4 + b], half)
        half = jnp.clip(half - POOL * (token % 2), 0, POOL)
        offset = place - token * POOL
        take = jnp.where((offset >= 0) & (offset < half), 1.0, 0.0).astype(BF)
        total = dot(take, normed)[:tokens]
        half_f = half[:tokens, :width].astype(F32)
        stage[pl.ds(i * tokens, tokens), :] = jnp.where(
            half_f > 0.0, total / jnp.maximum(half_f, 1.0), NO_TOKEN
        )

    def qkv_chunk(i):
        spot = pl.ds(i * chunk, chunk)
        joined = dot(nrm[spot, :], w_qkv[...])
        queries[spot, :] = (head_rms(joined[:, :width]) * q_scale).astype(BF)
        keys[spot, :] = head_rms(joined[:, width : 2 * width]).astype(BF)
        values[spot, :] = joined[:, 2 * width :].astype(BF)

    def copy_of(block, part, send_sem, seq, rep):
        share = pl.ds(part * part_rows, part_rows)
        return pltpu.make_async_remote_copy(
            src_ref=tokens_all.at[block, share],
            dst_ref=tokens_all.at[block, share],
            send_sem=send_sem,
            recv_sem=recv_sem.at[part, block],
            device_id={"seq": seq, "rep": rep},
            device_id_type=MESH,
        )

    def spread(part, step):
        return copy_of(me, part, direct_send.at[part, step], *place_of(step))

    def forward(part, block, step):
        return copy_of(block, part, pair_send.at[part, block, step], my_seq, partner_of(step))

    def arrival(part, block):
        return copy_of(block, part, direct_send.at[part, 0], *place_of(0))

    def publish(part):
        share = pl.ds(part * part_rows, part_rows)
        tokens_all[me, share] = stage[share, :].astype(BF)
        if part == 0:
            pl.semaphore_wait(barrier, direct + pair - 1)
        each(direct, 0, lambda step: spread(part, step).start())
        each(pair, 1, lambda step: forward(part, me, step).start())

    def block_of(step):
        seq, rep = place_of(direct - 1 - step)
        return seq * rep_n + rep

    def relay(step):
        block = block_of(step)
        for part in range(parts):
            arrival(part, block).wait_recv()
            each(pair, 1, lambda away: forward(part, block, away).start())

    gather_rows(0, chunk)
    for i in range(1, chunks):
        early = part_chunks == i - 1
        if early:
            publish(0)
        last = part_chunks == i + 0 and parts > 1
        gather_rows(i * chunk + (chunk // 2 if early else 0), chunk // 2 if early else chunk)
        pool_chunk(i - 1)
        if last:
            gather_rows((i + 1) * chunk, chunk // 2)
    pool_chunk(chunks - 1)
    publish(parts - 1)
    own_block = stage[...].astype(BF)

    for load in loads[1:]:
        load.wait()

    def ball_chunk(i):
        mixes = []
        for b in range(4):
            spot = pl.ds(i * chunk + b * BALL, BALL)
            q, k, v = queries[spot, :], keys[spot, :], values[spot, :]
            live = lax.broadcasted_iota(jnp.int32, (BALL, LANES), 0) < counts[i * 4 + b]
            there = jnp.where(live, 1.0, 0.0).astype(BF)
            alive = [there * lanes for lanes in head_lanes]
            ones = jnp.concatenate(alive, axis=0)
            slab_mixes = []
            for slab in slabs:
                weights = jnp.exp2(dot_t(q[:, slab], by_head(k[:, slab]))).astype(BF)
                seen = jnp.concatenate([v[:, slab] * lanes for lanes in alive], axis=0)
                mixed = dot(weights, jnp.concatenate([seen, ones], axis=1))
                slab_mixes.append((mixed[:, :LANES] / mixed[:, LANES:]).astype(BF))
            mixes.append(jnp.concatenate(slab_mixes, axis=1))
        fine = dot(jnp.concatenate(mixes, axis=0), w_out[...])
        spot = pl.ds(i * chunk, chunk)
        mid[spot, :] = (srt[spot, :].astype(F32) + fine).astype(BF)

    first = direct // 2
    qkv_chunk(0)
    for i in range(chunks):
        if i + 1 < chunks:
            qkv_chunk(i + 1)
        ball_chunk(i)
        if i == chunks - 2:
            each(first, 0, relay)
    each(direct, first, relay)

    own_tokens = jnp.where(own_block < NO_TOKEN / 2, own_block, 0.0).astype(BF)
    q_c = dot(own_tokens, c_qkv[:, :width])
    q_c = (head_rms(q_c) * lane_scale(1)).astype(BF)
    coarse_queries = [by_head(q_c[:, slab]) for slab in slabs]

    def gathered(part, step):
        rep = partner_of(step)
        each(pairs, 0, lambda away: each(seq_n, 0, lambda seq: arrival(
            part, seq * rep_n + lax.rem(rep + pair * away, rep_n)
        ).wait_recv()))

    blocks = seq_n * pairs
    group = math.gcd(blocks, 8)

    def coarse_keys(side, g):
        members = [
            (g * group + t) // pairs * rep_n + (g * group + t) % pairs * pair + side
            for t in range(group)
        ]
        block = jnp.concatenate([tokens_all[member] for member in members], axis=0)
        there = block < NO_TOKEN / 2
        ones = jnp.where(there[:, :LANES], 1.0, 0.0).astype(BF)
        joined = dot(jnp.where(there, block, 0.0).astype(BF), c_qkv[:, width:])
        c_keys = head_rms(joined[:, :width]).astype(BF)
        c_values = joined[:, width:].astype(BF)
        sums = []
        for query, slab in zip(coarse_queries, slabs):
            weights = jnp.exp2(dot_t(query, c_keys[:, slab])).astype(BF)
            sums.append(dot(weights, jnp.concatenate([c_values[:, slab], ones], axis=1)))
        return sums

    def coarse_side(side):
        if blocks == group:
            return coarse_keys(side, 0)
        return lax.fori_loop(
            0,
            blocks // group,
            lambda g, total: [a + b for a, b in zip(total, coarse_keys(side, g))],
            [jnp.zeros((near_heads * coarse_rows, 2 * LANES), F32) for _ in slabs],
        )

    sums = coarse_side(lax.rem(my_rep, pair))
    for part in range(parts):
        each(pair, 1, functools.partial(gathered, part))
    if pair > 1:
        sums = [a + b for a, b in zip(sums, coarse_side(lax.rem(my_rep + 1, pair)))]
    slab_mixes = []
    for total in sums:
        ratio = total[:, :LANES] / total[:, LANES:]
        mix = jnp.zeros((coarse_rows, LANES), F32)
        for h in range(near_heads):
            mix = jnp.where(near == h, ratio[h * coarse_rows : (h + 1) * coarse_rows], mix)
        slab_mixes.append(mix)
    mix = jnp.concatenate(slab_mixes, axis=1)
    coarse[...] = dot(mix.astype(BF), c_out[...])

    for part in range(parts):
        each(direct, 0, lambda step: spread(part, step).wait_send())
        each(pair, 1, lambda step: forward(part, me, step).wait_send())
        each(direct, 0, lambda step: each(
            pair, 1, lambda away: forward(part, block_of(step), away).wait_send()
        ))


def mlp_kernel(
    mid,
    coarse,
    order,
    gain_mlp,
    w_up,
    w_down,
    out,
    res,
    ready,
    packed,
    order_twice,
    spots,
    load_sem,
    out_sem,
):
    rows, width = mid.shape
    chunk = 4 * BALL
    chunks = rows // chunk
    tokens = chunk // POOL
    gain_half = gain_mlp[...] * 0.5

    order_twice[...] = order[...] * 2
    load_spots = pltpu.make_async_copy(order_twice, spots, load_sem)
    load_spots.start()

    def mlp_chunk(i):
        terms = coarse[pl.ds(i * tokens, tokens), :]
        spread = jnp.concatenate(
            [jnp.broadcast_to(terms[t : t + 1], (POOL, width)) for t in range(tokens)], axis=0
        )
        middle = mid[pl.ds(i * chunk, chunk), :].astype(F32) + spread
        mlp_in = rms(middle, gain_half).astype(BF)
        activated = gelu_of_half(dot(mlp_in, w_up[...]).astype(BF))
        result = middle + dot(activated, w_down[...])
        for n in range(width // LANES):
            res[pl.ds(2 * i * chunk + n, chunk, stride=2), :] = result[:, n * LANES : (n + 1) * LANES]

    def scatter_chunk(i):
        for r in range(i * chunk, (i + 1) * chunk):
            ready[pl.ds(spots[0, r], 2), :] = res[pl.ds(2 * r, 2), :]

    mlp_chunk(0)
    load_spots.wait()
    for i in range(1, chunks):
        scatter_chunk(i - 1)
        mlp_chunk(i)
    scatter_chunk(chunks - 1)

    def leave(i):
        spot = pl.ds(i * chunk, chunk)
        return pltpu.make_async_copy(packed.at[spot, :], out.at[spot, :], out_sem.at[i])

    for i in range(chunks):
        packed[pl.ds(i * chunk, chunk), :] = jnp.concatenate(
            [ready[pl.ds(2 * i * chunk + n, chunk, stride=2), :] for n in range(width // LANES)], axis=1
        ).astype(BF)
        leave(i).start()
    for i in range(chunks):
        leave(i).wait()


def on_device(
    sizes,
    points,
    ball_order,
    ball_counts,
    gain_attn,
    gain_mlp,
    head_temps,
    w_qkv,
    w_out,
    c_qkv,
    c_out,
    w_up,
    w_down,
):
    rows, width = points.shape
    heads = head_temps.shape[1]
    seq_n, rep_n = sizes
    peers = seq_n * rep_n
    coarse_rows = rows // POOL
    chunks = rows // (4 * BALL)
    vmem = pl.BlockSpec(memory_space=pltpu.VMEM)
    hbm = pl.BlockSpec(memory_space=pltpu.HBM)
    far = pl.BlockSpec(memory_space=pl.ANY)
    dma = pltpu.SemaphoreType.DMA
    tall = rows * width // LANES
    mid, coarse, gain_mid = pl.pallas_call(
        functools.partial(attend_kernel, (*sizes, heads)),
        out_shape=(
            jax.ShapeDtypeStruct((rows, width), BF),
            jax.ShapeDtypeStruct((coarse_rows, width), F32),
            jax.ShapeDtypeStruct((1, width), F32),
        ),
        in_specs=[hbm] * 10,
        out_specs=(vmem,) * 3,
        scratch_shapes=[
            pltpu.VMEM((rows, width), BF),
            pltpu.VMEM((1, rows), jnp.int32),
            pltpu.VMEM((1, rows), jnp.int32),
            pltpu.VMEM((1, width), F32),
            pltpu.SMEM((1, rows), jnp.int32),
            pltpu.SMEM(ball_counts.shape, jnp.int32),
            pltpu.SMEM(head_temps.shape, F32),
            pltpu.VMEM((tall, LANES), F32),
            pltpu.VMEM((tall, LANES), F32),
            pltpu.VMEM((rows, width), BF),
            pltpu.VMEM((rows, width), BF),
            pltpu.VMEM((rows, width), BF),
            pltpu.VMEM((rows, width), BF),
            pltpu.VMEM((rows, width), BF),
            pltpu.VMEM((coarse_rows, width), F32),
            pltpu.VMEM((peers, coarse_rows, width), BF),
            pltpu.VMEM(w_qkv.shape, BF),
            pltpu.VMEM(w_out.shape, BF),
            pltpu.VMEM(c_qkv.shape, BF),
            pltpu.VMEM(c_out.shape, BF),
            dma((chunks,)),
            dma((10,)),
            dma((2, peers)),
            dma((2, peers, 2)),
            dma((2, peers)),
        ],
        compiler_params=pltpu.CompilerParams(
            collective_id=0, has_side_effects=True, vmem_limit_bytes=VMEM_ATTEND
        ),
        name="attend",
    )(
        *(
            pltpu.with_memory_space_constraint(operand, pltpu.HBM)
            for operand in (
                points,
                ball_order,
                ball_counts,
                gain_attn.reshape(1, width),
                head_temps,
                w_qkv,
                w_out,
                c_qkv,
                c_out,
                gain_mlp.reshape(1, width),
            )
        )
    )
    return pl.pallas_call(
        mlp_kernel,
        out_shape=jax.ShapeDtypeStruct(points.shape, points.dtype),
        in_specs=[vmem] * 6,
        out_specs=far,
        scratch_shapes=[
            pltpu.VMEM((tall, LANES), F32),
            pltpu.VMEM((tall, LANES), F32),
            pltpu.VMEM((rows, width), BF),
            pltpu.VMEM((1, rows), jnp.int32),
            pltpu.SMEM((1, rows), jnp.int32),
            dma,
            dma((chunks,)),
        ],
        compiler_params=pltpu.CompilerParams(vmem_limit_bytes=VMEM_MLP),
        name="mlp",
    )(mid, coarse, ball_order, gain_mid, w_up, w_down)


def solution(mesh):
    rows = P(("groups", "seq", "rep"))
    sizes = (mesh.shape["seq"], mesh.shape["rep"])
    return jax.shard_map(
        functools.partial(on_device, sizes),
        mesh=mesh,
        in_specs=(P(("groups", "seq", "rep"), None),) * 2 + (rows,) + (P(),) * 9,
        out_specs=P(("groups", "seq", "rep"), None),
        check_vma=False,
    )
```

```python
import functools
import math

import jax
import jax.numpy as jnp
from jax import lax
from jax.experimental import pallas as pl
from jax.experimental.pallas import tpu as pltpu
from jax.sharding import PartitionSpec as P

BALL = 128
POOL = 64
EPS = 1e-06
VMEM_ATTEND = 32 << 20
VMEM_MLP = 32 << 20
LANES = 128
GELU_A = math.sqrt(2.0 / math.pi)
GELU_B = 0.044715 * math.sqrt(2.0 / math.pi)
NO_TOKEN = 1024.0
LOG2E = 1.4426950408889634
MESH = pl.DeviceIdType.MESH
BF = jnp.bfloat16
F32 = jnp.float32


def dot(a, b):
    return jnp.dot(a, b, preferred_element_type=F32)


def dot_t(a, b):
    return lax.dot_general(a, b, (((1,), (1,)), ((), ())), preferred_element_type=F32)


def gelu_of_half(half):
    inner = half * (2.0 * GELU_A + 8.0 * GELU_B * (half * half))
    return half + half * jnp.tanh(inner)


def rms(values, gain):
    return values * lax.rsqrt(jnp.mean(values * values, axis=-1, keepdims=True) + EPS) * gain


def attend_kernel(
    sizes,
    points_hbm,
    order_hbm,
    counts_hbm,
    gain_hbm,
    temps_hbm,
    w_qkv_hbm,
    w_out_hbm,
    c_qkv_hbm,
    c_out_hbm,
    gain_mlp_hbm,
    mid,
    coarse,
    gain_mid,
    points,
    order,
    order_twice,
    gain_attn,
    spots,
    counts,
    temps,
    wide,
    picked,
    srt,
    nrm,
    queries,
    keys,
    values,
    stage,
    tokens_all,
    w_qkv,
    w_out,
    c_qkv,
    c_out,
    points_sem,
    load_sem,
    direct_send,
    pair_send,
    recv_sem,
):
    seq_n, rep_n, heads = sizes
    peers = seq_n * rep_n
    rows, width = points.shape
    head_dim = width // heads
    chunk = 4 * BALL
    chunks = rows // chunk
    tokens = chunk // POOL
    coarse_rows = rows // POOL
    halves = width // LANES
    my_seq = lax.axis_index("seq")
    my_rep = lax.axis_index("rep")
    me = my_seq * rep_n + my_rep
    pair = 2 if rep_n % 2 == 0 else 1
    pairs = rep_n // pair
    direct = seq_n * pairs - 1

    small = [
        pltpu.make_async_copy(source, target, load_sem.at[n])
        for n, (source, target) in enumerate(
            [(order_hbm, order), (counts_hbm, counts), (temps_hbm, temps), (gain_hbm, gain_attn)]
        )
    ]
    loads = [
        pltpu.make_async_copy(source, target, load_sem.at[4 + n])
        for n, (source, target) in enumerate(
            [
                (w_qkv_hbm, w_qkv),
                (w_out_hbm, w_out),
                (c_qkv_hbm, c_qkv),
                (c_out_hbm, c_out),
                (gain_mlp_hbm, gain_mid),
            ]
        )
    ]
    load_spots = pltpu.make_async_copy(order_twice, spots, load_sem.at[9])

    def enter(i):
        spot = pl.ds(i * chunk, chunk)
        return pltpu.make_async_copy(points_hbm.at[spot, :], points.at[spot, :], points_sem.at[i])

    small[0].start()
    for i in range(chunks):
        enter(i).start()
    for load in small[1:] + loads:
        load.start()

    barrier = pltpu.get_barrier_semaphore()

    def each(count, first, act):
        def body(step, carry):
            act(step)
            return carry

        lax.fori_loop(first, count, body, 0)

    def seq_place(step):
        above = seq_n - 1 - my_seq
        rising = jnp.where(step < above, seq_n - 1 - step, step - above)
        falling = jnp.where(step < my_seq, step, seq_n - 1 - step + my_seq)
        return jnp.where(my_seq < seq_n // 2, rising, falling)

    def place_of(step):
        away = step // pairs
        seq = jnp.where(away < seq_n - 1, seq_place(away), my_seq)
        rep = lax.rem(my_rep + pair * (1 + lax.rem(step, pairs)), rep_n)
        return seq, rep

    def partner_of(step):
        return my_rep - lax.rem(my_rep, pair) + lax.rem(my_rep + step, pair)

    def greet(seq, rep):
        pl.semaphore_signal(
            barrier, inc=1, device_id={"seq": seq, "rep": rep}, device_id_type=MESH
        )

    each(direct, 0, lambda step: greet(*place_of(step)))
    each(pair, 1, lambda step: greet(my_seq, partner_of(step)))

    small[0].wait()
    order_twice[...] = order[...] * 2
    load_spots.start()

    lane_head = lax.broadcasted_iota(jnp.int32, (1, width), 1) // head_dim
    near_heads = LANES // head_dim
    slabs = [slice(g * LANES, (g + 1) * LANES) for g in range(width // LANES)]
    near = lax.broadcasted_iota(jnp.int32, (1, LANES), 1) // head_dim
    head_lanes = [(near == h).astype(F32).astype(BF) for h in range(near_heads)]

    def by_head(block):
        return jnp.concatenate([block * lanes for lanes in head_lanes], axis=0)

    block_mean = jnp.where(
        lax.broadcasted_iota(jnp.int32, (width, width), 0) // head_dim
        == lax.broadcasted_iota(jnp.int32, (width, width), 1) // head_dim,
        1.0 / head_dim,
        0.0,
    ).astype(BF)

    def lane_scale(row):
        scale = jnp.zeros((1, width), F32)
        for h in range(heads):
            scale = jnp.where(lane_head == h, temps[row, h], scale)
        return scale * (LOG2E / math.sqrt(head_dim))

    def head_rms(values):
        return values * lax.rsqrt(dot((values * values).astype(BF), block_mean) + EPS)

    for i in range(chunks):
        enter(i).wait()
        block = points[pl.ds(i * chunk, chunk), :].astype(F32)
        for n in range(halves):
            wide[pl.ds(2 * i * chunk + n, chunk, stride=2), :] = block[:, slabs[n]]
    for load in small[1:]:
        load.wait()
    load_spots.wait()
    loads[0].wait()

    gain_a = gain_attn[...]
    q_scale = lane_scale(0)

    def gather_chunk(i):
        for r in range(i * chunk, (i + 1) * chunk):
            picked[pl.ds(2 * r, 2), :] = wide[pl.ds(spots[0, r], 2), :]

    def pool_chunk(i):
        sorted_rows = jnp.concatenate(
            [picked[pl.ds(2 * i * chunk + n, chunk, stride=2), :] for n in range(halves)], axis=1
        )
        spot = pl.ds(i * chunk, chunk)
        srt[spot, :] = sorted_rows.astype(BF)
        normed = rms(sorted_rows, gain_a).astype(BF)
        nrm[spot, :] = normed
        shape = (2 * tokens, chunk)
        token = lax.broadcasted_iota(jnp.int32, shape, 0)
        place = lax.broadcasted_iota(jnp.int32, shape, 1)
        half = jnp.zeros(shape, jnp.int32)
        for b in range(4):
            half = jnp.where(token // 2 == b, counts[i * 4 + b], half)
        half = jnp.clip(half - POOL * (token % 2), 0, POOL)
        offset = place - token * POOL
        take = jnp.where((offset >= 0) & (offset < half), 1.0, 0.0).astype(BF)
        total = dot(take, normed)[:tokens]
        half_f = half[:tokens, :width].astype(F32)
        stage[pl.ds(i * tokens, tokens), :] = jnp.where(
            half_f > 0.0, total / jnp.maximum(half_f, 1.0), NO_TOKEN
        )

    def qkv_chunk(i):
        spot = pl.ds(i * chunk, chunk)
        joined = dot(nrm[spot, :], w_qkv[...])
        queries[spot, :] = (head_rms(joined[:, :width]) * q_scale).astype(BF)
        keys[spot, :] = head_rms(joined[:, width : 2 * width]).astype(BF)
        values[spot, :] = joined[:, 2 * width :].astype(BF)

    gather_chunk(0)
    for i in range(1, chunks):
        gather_chunk(i)
        pool_chunk(i - 1)
    pool_chunk(chunks - 1)

    own_block = stage[...].astype(BF)
    tokens_all[me] = own_block

    pl.semaphore_wait(barrier, direct + pair - 1)

    def copy_of(block, send_sem, seq, rep):
        return pltpu.make_async_remote_copy(
            src_ref=tokens_all.at[block],
            dst_ref=tokens_all.at[block],
            send_sem=send_sem,
            recv_sem=recv_sem.at[block],
            device_id={"seq": seq, "rep": rep},
            device_id_type=MESH,
        )

    def spread(step):
        return copy_of(me, direct_send.at[step], *place_of(step))

    def forward(block, step):
        return copy_of(block, pair_send.at[block, step], my_seq, partner_of(step))

    def arrival(block):
        return copy_of(block, direct_send.at[0], *place_of(0))

    each(direct, 0, lambda step: spread(step).start())
    each(pair, 1, lambda step: forward(me, step).start())

    def block_of(step):
        seq, rep = place_of(direct - 1 - step)
        return seq * rep_n + rep

    def relay(step):
        block = block_of(step)
        arrival(block).wait_recv()
        each(pair, 1, lambda away: forward(block, away).start())

    for load in loads[1:]:
        load.wait()

    def ball_chunk(i):
        mixes = []
        for b in range(4):
            spot = pl.ds(i * chunk + b * BALL, BALL)
            q, k, v = queries[spot, :], keys[spot, :], values[spot, :]
            live = lax.broadcasted_iota(jnp.int32, (BALL, LANES), 0) < counts[i * 4 + b]
            there = jnp.where(live, 1.0, 0.0).astype(BF)
            alive = [there * lanes for lanes in head_lanes]
            ones = jnp.concatenate(alive, axis=0)
            slab_mixes = []
            for slab in slabs:
                weights = jnp.exp2(dot_t(q[:, slab], by_head(k[:, slab]))).astype(BF)
                seen = jnp.concatenate([v[:, slab] * lanes for lanes in alive], axis=0)
                mixed = dot(weights, jnp.concatenate([seen, ones], axis=1))
                slab_mixes.append((mixed[:, :LANES] / mixed[:, LANES:]).astype(BF))
            mixes.append(jnp.concatenate(slab_mixes, axis=1))
        fine = dot(jnp.concatenate(mixes, axis=0), w_out[...])
        spot = pl.ds(i * chunk, chunk)
        mid[spot, :] = (srt[spot, :].astype(F32) + fine).astype(BF)

    qkv_chunk(0)
    for i in range(chunks):
        if i + 1 < chunks:
            qkv_chunk(i + 1)
        ball_chunk(i)
    each(direct, 0, relay)

    own_tokens = jnp.where(own_block < NO_TOKEN / 2, own_block, 0.0).astype(BF)
    q_c = dot(own_tokens, c_qkv[:, :width])
    q_c = (head_rms(q_c) * lane_scale(1)).astype(BF)
    coarse_queries = [by_head(q_c[:, slab]) for slab in slabs]

    def gathered(step):
        rep = partner_of(step)
        each(pairs, 0, lambda away: each(seq_n, 0, lambda seq: arrival(
            seq * rep_n + lax.rem(rep + pair * away, rep_n)
        ).wait_recv()))

    blocks = seq_n * pairs
    group = math.gcd(blocks, 8)

    def coarse_keys(side, g):
        members = [
            (g * group + t) // pairs * rep_n + (g * group + t) % pairs * pair + side
            for t in range(group)
        ]
        block = jnp.concatenate([tokens_all[member] for member in members], axis=0)
        there = block < NO_TOKEN / 2
        ones = jnp.where(there[:, :LANES], 1.0, 0.0).astype(BF)
        joined = dot(jnp.where(there, block, 0.0).astype(BF), c_qkv[:, width:])
        c_keys = head_rms(joined[:, :width]).astype(BF)
        c_values = joined[:, width:].astype(BF)
        sums = []
        for query, slab in zip(coarse_queries, slabs):
            weights = jnp.exp2(dot_t(query, c_keys[:, slab])).astype(BF)
            sums.append(dot(weights, jnp.concatenate([c_values[:, slab], ones], axis=1)))
        return sums

    def coarse_side(side):
        if blocks == group:
            return coarse_keys(side, 0)
        return lax.fori_loop(
            0,
            blocks // group,
            lambda g, total: [a + b for a, b in zip(total, coarse_keys(side, g))],
            [jnp.zeros((near_heads * coarse_rows, 2 * LANES), F32) for _ in slabs],
        )

    sums = coarse_side(lax.rem(my_rep, pair))
    each(pair, 1, gathered)
    if pair > 1:
        sums = [a + b for a, b in zip(sums, coarse_side(lax.rem(my_rep + 1, pair)))]
    slab_mixes = []
    for total in sums:
        ratio = total[:, :LANES] / total[:, LANES:]
        mix = jnp.zeros((coarse_rows, LANES), F32)
        for h in range(near_heads):
            mix = jnp.where(near == h, ratio[h * coarse_rows : (h + 1) * coarse_rows], mix)
        slab_mixes.append(mix)
    mix = jnp.concatenate(slab_mixes, axis=1)
    coarse[...] = dot(mix.astype(BF), c_out[...])

    each(direct, 0, lambda step: spread(step).wait_send())
    each(pair, 1, lambda step: forward(me, step).wait_send())
    each(direct, 0, lambda step: each(
        pair, 1, lambda away: forward(block_of(step), away).wait_send()
    ))


def mlp_kernel(
    mid,
    coarse,
    order,
    gain_mlp,
    w_up,
    w_down,
    out,
    res,
    ready,
    packed,
    order_twice,
    spots,
    load_sem,
    out_sem,
):
    rows, width = mid.shape
    chunk = 4 * BALL
    chunks = rows // chunk
    tokens = chunk // POOL
    gain_half = gain_mlp[...] * 0.5

    order_twice[...] = order[...] * 2
    load_spots = pltpu.make_async_copy(order_twice, spots, load_sem)
    load_spots.start()

    def mlp_chunk(i):
        terms = coarse[pl.ds(i * tokens, tokens), :]
        spread = jnp.concatenate(
            [jnp.broadcast_to(terms[t : t + 1], (POOL, width)) for t in range(tokens)], axis=0
        )
        middle = mid[pl.ds(i * chunk, chunk), :].astype(F32) + spread
        mlp_in = rms(middle, gain_half).astype(BF)
        activated = gelu_of_half(dot(mlp_in, w_up[...]).astype(BF))
        result = middle + dot(activated, w_down[...])
        for n in range(width // LANES):
            res[pl.ds(2 * i * chunk + n, chunk, stride=2), :] = result[:, n * LANES : (n + 1) * LANES]

    def scatter_chunk(i):
        for r in range(i * chunk, (i + 1) * chunk):
            ready[pl.ds(spots[0, r], 2), :] = res[pl.ds(2 * r, 2), :]

    mlp_chunk(0)
    load_spots.wait()
    for i in range(1, chunks):
        scatter_chunk(i - 1)
        mlp_chunk(i)
    scatter_chunk(chunks - 1)

    share = chunk // 2
    shares = rows // share

    def leave(i):
        spot = pl.ds(i * share, share)
        return pltpu.make_async_copy(packed.at[spot, :], out.at[spot, :], out_sem.at[i])

    for i in range(shares):
        packed[pl.ds(i * share, share), :] = jnp.concatenate(
            [ready[pl.ds(2 * i * share + n, share, stride=2), :] for n in range(width // LANES)], axis=1
        ).astype(BF)
        leave(i).start()
    for i in range(shares):
        leave(i).wait()


def on_device(
    sizes,
    points,
    ball_order,
    ball_counts,
    gain_attn,
    gain_mlp,
    head_temps,
    w_qkv,
    w_out,
    c_qkv,
    c_out,
    w_up,
    w_down,
):
    rows, width = points.shape
    heads = head_temps.shape[1]
    seq_n, rep_n = sizes
    peers = seq_n * rep_n
    coarse_rows = rows // POOL
    chunks = rows // (4 * BALL)
    vmem = pl.BlockSpec(memory_space=pltpu.VMEM)
    hbm = pl.BlockSpec(memory_space=pltpu.HBM)
    far = pl.BlockSpec(memory_space=pl.ANY)
    dma = pltpu.SemaphoreType.DMA
    tall = rows * width // LANES
    mid, coarse, gain_mid = pl.pallas_call(
        functools.partial(attend_kernel, (*sizes, heads)),
        out_shape=(
            jax.ShapeDtypeStruct((rows, width), BF),
            jax.ShapeDtypeStruct((coarse_rows, width), F32),
            jax.ShapeDtypeStruct((1, width), F32),
        ),
        in_specs=[hbm] * 10,
        out_specs=(vmem,) * 3,
        scratch_shapes=[
            pltpu.VMEM((rows, width), BF),
            pltpu.VMEM((1, rows), jnp.int32),
            pltpu.VMEM((1, rows), jnp.int32),
            pltpu.VMEM((1, width), F32),
            pltpu.SMEM((1, rows), jnp.int32),
            pltpu.SMEM(ball_counts.shape, jnp.int32),
            pltpu.SMEM(head_temps.shape, F32),
            pltpu.VMEM((tall, LANES), F32),
            pltpu.VMEM((tall, LANES), F32),
            pltpu.VMEM((rows, width), BF),
            pltpu.VMEM((rows, width), BF),
            pltpu.VMEM((rows, width), BF),
            pltpu.VMEM((rows, width), BF),
            pltpu.VMEM((rows, width), BF),
            pltpu.VMEM((coarse_rows, width), F32),
            pltpu.VMEM((peers, coarse_rows, width), BF),
            pltpu.VMEM(w_qkv.shape, BF),
            pltpu.VMEM(w_out.shape, BF),
            pltpu.VMEM(c_qkv.shape, BF),
            pltpu.VMEM(c_out.shape, BF),
            dma((chunks,)),
            dma((10,)),
            dma((peers,)),
            dma((peers, 2)),
            dma((peers,)),
        ],
        compiler_params=pltpu.CompilerParams(
            collective_id=0, has_side_effects=True, vmem_limit_bytes=VMEM_ATTEND
        ),
        name="attend",
    )(
        *(
            pltpu.with_memory_space_constraint(operand, pltpu.HBM)
            for operand in (
                points,
                ball_order,
                ball_counts,
                gain_attn.reshape(1, width),
                head_temps,
                w_qkv,
                w_out,
                c_qkv,
                c_out,
                gain_mlp.reshape(1, width),
            )
        )
    )
    return pl.pallas_call(
        mlp_kernel,
        out_shape=jax.ShapeDtypeStruct(points.shape, points.dtype),
        in_specs=[vmem] * 6,
        out_specs=far,
        scratch_shapes=[
            pltpu.VMEM((tall, LANES), F32),
            pltpu.VMEM((tall, LANES), F32),
            pltpu.VMEM((rows, width), BF),
            pltpu.VMEM((1, rows), jnp.int32),
            pltpu.SMEM((1, rows), jnp.int32),
            dma,
            dma((2 * chunks,)),
        ],
        compiler_params=pltpu.CompilerParams(vmem_limit_bytes=VMEM_MLP),
        name="mlp",
    )(mid, coarse, ball_order, gain_mid, w_up, w_down)


def solution(mesh):
    rows = P(("groups", "seq", "rep"))
    sizes = (mesh.shape["seq"], mesh.shape["rep"])
    return jax.shard_map(
        functools.partial(on_device, sizes),
        mesh=mesh,
        in_specs=(P(("groups", "seq", "rep"), None),) * 2 + (rows,) + (P(),) * 9,
        out_specs=P(("groups", "seq", "rep"), None),
        check_vma=False,
    )
```
